512 devices in a mesh: lon: 32 (over z_lo, y), lat: 4 (over x), ens: 4 (over z_hi, core).
Axes of the slice: x: 4, y: 4, z: 16 (z_hi: 2, z_lo: 8; z = z_hi * 8 + z_lo), core: 2. Of those that a mesh axis runs over, the one named last changes fastest.
Arguments:
- obs_values: bfloat16 [4, 32768, 256], P('ens', ('lon', 'lat')), may hold values from -6 to 6
- obs_tile: int32 [4, 32768, 1], P('ens', ('lon', 'lat')), may hold values from 0 to 127; in each aligned block of 256 rows (0 to 255, 256 to 511, ..., all dimensions but the last counted through in order) at most 4 rows name the same one
- obs_cell: int32 [4, 32768], P('ens', ('lon', 'lat')), may hold values from 0 to 255
- backdrop: bfloat16 [4, 32, 1024, 256], P('ens', 'lat', 'lon'), may hold values from -6 to 6
- seed_grad: bfloat16 [4, 32, 1024, 256], P('ens', 'lat', 'lon'), may hold values from -6 to 6
- kernels: float32 [4, 9, 256], replicated, may hold values from -1.5 to 1.5
- weights: bfloat16 [4, 256, 256], replicated, may hold values from -0.375 to 0.375
Outputs:
- state: bfloat16 [4, 32, 1024, 256], P('ens', 'lat', 'lon')
- weight_grad: float32 [4, 256, 256], replicated
- kernel_grad: float32 [4, 9, 256], replicated
- obs_grad: bfloat16 [4, 32768, 256], P('ens', ('lon', 'lat'))
The draws below stay inside these ranges and needn't reach their ends.
Inputs may be any that keep to these rules, and one draw needn't show every extreme that they name: `obs_tile`: among the 256 observations of one device no tile is named more than 4 times, a bound that some block reaches.
All inputs are finite; a program needn't handle non-finite values.
Results may differ from the reference program's by a relative error of at most 0.012.
Values may be sent and summed in bfloat16 or wider, within the bound.
A program may use at most 64 MiB of HBM per device.

```python
import math
import jax
import jax.numpy as jnp
import numpy as np
from jax import lax

C = 256
LAYERS = 4
LAT_DEV = 8
LON_DEV = 32
OBS_DEV = 256
SPATIAL = 128
CAP = 4
CELLS = 256
ENS = 4
NLAT = 32
NLON = 1024
OBS = 32768
N_LAT = 4


def set_ends(values, stream_key, least, largest):
    longest = values.shape.index(max(values.shape))
    spots = []
    for shift in (0, 1):
        where = [jax.random.randint(jax.random.fold_in(stream_key, axis), (), 0, length) for axis, length in enumerate(values.shape)]
        where[longest] = (where[longest] + shift) % values.shape[longest]
        spots.append(tuple(where))
    return values.at[spots[0]].set(least).at[spots[1]].set(largest)


def block_levels(stream_key, extent, pieces, least, high):
    def one(position, shards_of):
        heights = jax.random.uniform(jax.random.fold_in(jax.random.fold_in(stream_key, 6), position), (shards_of,), jnp.float32, least / len(pieces), high / len(pieces))
        return jnp.repeat(jnp.exp(heights), extent[position] // shards_of).reshape((-1,) + (1,) * (len(extent) - position - 1))

    loudness = one(*pieces[0])
    for cut in pieces[1:]:
        loudness = loudness * one(*cut)
    return loudness


def assign_block(rng, own, number, rows, count, top, most, lean):
    sequence = jax.random.permutation(rng, count)
    crowded, ordinary = load_shares(count, rows * top, most, lean, True), load_shares(count, rows * top, most, lean, False)
    places = jnp.arange(count)

    def named(sizes, turn):
        used = int((sizes > 0).sum())
        fixed = max(1, used // 4)
        moved = fixed + (places - fixed + turn * (used - fixed)) % max(1, count - fixed)
        return jnp.zeros((count,), jnp.int32).at[sequence[jnp.where(places < fixed, places, moved)]].set(jnp.asarray(sizes, jnp.int32))

    sizes = jnp.where(number % 4 == 0, named(crowded, number // 4), named(ordinary, number - number // 4 - 1))
    mixed = jax.random.permutation(jax.random.fold_in(own, 3), count)
    source_of, receiver = mixed[0:count // 2 * 2:2], mixed[1:count // 2 * 2:2]
    slack = jnp.minimum(sizes[source_of] - 1, most - sizes[receiver]) // 2
    slack = jnp.where((source_of == sequence[0]) | (receiver == sequence[0]) | (sizes[receiver] == 0), 0, jnp.maximum(slack, 0))
    moved = jax.random.randint(jax.random.fold_in(own, 4), (count // 2,), 0, 1 << 20) % (slack + 1)
    sizes = sizes.at[source_of].add(-moved).at[receiver].add(moved)
    labels = jnp.searchsorted(jnp.cumsum(sizes), jnp.arange(rows * top), side="right").astype(jnp.int32)
    table = labels.reshape(top, rows).T
    table = table[jax.random.permutation(jax.random.fold_in(own, 1), rows)]
    turn = jax.random.randint(jax.random.fold_in(own, 2), (rows, 1), 0, top)
    return jnp.take_along_axis(table, (jnp.arange(top)[None, :] + turn) % top, axis=1)


def load_shares(amount, total, reach, lean, full):
    portions = [(1 << 20) // math.isqrt(standing ** lean) + 1 for standing in range(1, amount + 1)]
    largest = reach if full else min(reach, max(-(-total // amount), total * portions[0] // sum(portions)))
    least = 1 if total - largest >= amount - 1 else 0
    given, surplus = [largest] + [least] * (amount - 1), total - largest - least * (amount - 1)
    while surplus > 0:
        candidates = [i for i in range(1, amount) if given[i] < largest] or [i for i in range(1, amount) if given[i] < reach]
        pool, budget = sum([portions[i] for i in candidates]), surplus
        for i in candidates:
            more = min(reach - given[i], max(1, budget * portions[i] // pool), surplus)
            given[i] = given[i] + more
            surplus = surplus - more
    return np.array(given)


def centred(rng, shape, spread, most, pieces=(), dtype=jnp.bfloat16):
    drawn = jax.random.normal(rng, shape, jnp.float32) * spread
    if len(pieces) > 0:
        drawn = block_levels(rng, shape, pieces, -0.22, 0.18) * drawn
    return jnp.clip(drawn, min=-most, max=most).astype(dtype)


def setup_inputs(seed: int = 0) -> dict:
    key_list = jax.random.split(jax.random.key(seed), 8)
    obs_values = centred(key_list[0], (ENS, OBS, C), 1.0, 6.0, ((0, 4), (1, 128)))
    obs_tile_keys = jax.random.split(jax.random.fold_in(key_list[1], 1), ENS * OBS // OBS_DEV)
    obs_tile_turns = jax.random.permutation(jax.random.fold_in(key_list[1], 3), ENS * OBS // OBS_DEV)
    obs_tile = jax.vmap(lambda own, number: assign_block(jax.random.fold_in(key_list[1], 2), own, number, OBS_DEV, SPATIAL, 1, CAP, 2))(obs_tile_keys, obs_tile_turns).reshape((ENS, OBS, 1))
    obs_cell = set_ends(jax.random.randint(key_list[2], (ENS, OBS), 0, CELLS), jax.random.fold_in(key_list[2], 1), 0, CELLS - 1).astype(jnp.int32)
    backdrop = centred(key_list[3], (ENS, NLAT, NLON, C), 1.0, 6.0, ((0, 4), (1, 4), (2, 32)))
    seed_grad = centred(key_list[4], (ENS, NLAT, NLON, C), 1.0, 6.0, ((0, 4), (1, 4), (2, 32)))
    kernels = centred(key_list[5], (LAYERS, 9, C), 0.33, 1.5, (), jnp.float32)
    weights = centred(key_list[6], (LAYERS, C, C), C ** -0.5, 0.375)
    return {"obs_values": obs_values, "obs_tile": obs_tile, "obs_cell": obs_cell, "backdrop": backdrop, "seed_grad": seed_grad, "kernels": kernels, "weights": weights}


def pad_field(field):
    field = jnp.pad(field, ((1, 1), (0, 0), (0, 0)))
    return jnp.concatenate([field[:, -1:], field, field[:, :1]], axis=1)

def depthwise(padded, kernel_rows, offset, sign):
    rows = padded.shape[0] - 2
    cols = padded.shape[1] - 2
    accum = jnp.zeros((rows, cols, padded.shape[2]), jnp.float32)
    for a in range(3):
        for b in range(3):
            row_off = offset + sign * a
            col_off = offset + sign * b
            accum = accum + kernel_rows[3 * a + b] * padded[row_off:row_off + rows, col_off:col_off + cols].astype(jnp.float32)
    return accum

def reference(obs_values, obs_tile, obs_cell, backdrop, seed_grad, kernels, weights):
    inv_scale = 1.0 / math.sqrt(ENS * NLAT * NLON)

    def one_member(member):
        values, target, cell_ids, base, upstream = member
        target = target[:, 0]
        lon_tile = target // N_LAT
        lat_tile = target % N_LAT
        flat_cell = ((lat_tile * LAT_DEV + cell_ids // LON_DEV) * NLON + lon_tile * LON_DEV + cell_ids % LON_DEV).astype(jnp.int32)
        summed = jax.ops.segment_sum(values.astype(jnp.float32), flat_cell, num_segments=NLAT * NLON)
        counts = jax.ops.segment_sum(jnp.ones_like(flat_cell), flat_cell, num_segments=NLAT * NLON)
        divisor = jnp.maximum(counts, 1).astype(jnp.float32)[:, None]
        hidden = (base.reshape(-1, C).astype(jnp.float32) + summed / divisor).astype(jnp.bfloat16).reshape(NLAT, NLON, C)
        pads, pre_acts, acts = ([], [], [])
        for layer_idx in range(LAYERS):
            padded = pad_field(hidden)
            pre = depthwise(padded, kernels[layer_idx], 0, 1)
            act = jax.nn.silu(pre).astype(jnp.bfloat16)
            mixed = jnp.dot(act.reshape(-1, C), weights[layer_idx], preferred_element_type=jnp.float32)
            hidden = (hidden.astype(jnp.float32) + mixed.reshape(NLAT, NLON, C)).astype(jnp.bfloat16)
            pads.append(padded)
            pre_acts.append(pre)
            acts.append(act)
        grad = upstream.astype(jnp.float32) * inv_scale
        wgrads = [None] * LAYERS
        kgrads = [None] * LAYERS
        for layer_idx in reversed(range(LAYERS)):
            grad_bf = grad.astype(jnp.bfloat16).reshape(-1, C)
            wgrads[layer_idx] = lax.dot_general(acts[layer_idx].reshape(-1, C), grad_bf, (((0,), (0,)), ((), ())), preferred_element_type=jnp.float32)
            grad_act = lax.dot_general(grad_bf, weights[layer_idx], (((1,), (1,)), ((), ())), preferred_element_type=jnp.float32)
            pre = pre_acts[layer_idx]
            sig = jax.nn.sigmoid(pre)
            grad_pre = (grad_act.reshape(NLAT, NLON, C) * (sig * (1.0 + pre * (1.0 - sig)))).astype(jnp.bfloat16)
            padded = pads[layer_idx]
            taps = []
            for a in range(3):
                for b in range(3):
                    taps.append(lax.optimization_barrier(jnp.sum(grad_pre.astype(jnp.float32) * padded[a:a + NLAT, b:b + NLON].astype(jnp.float32), axis=(0, 1))))
            kgrads[layer_idx] = jnp.stack(taps)
            grad = grad + depthwise(pad_field(grad_pre), kernels[layer_idx], 2, -1)
        cell_grad = (grad.reshape(-1, C) / divisor).astype(jnp.bfloat16)
        return (hidden, jnp.stack(wgrads), jnp.stack(kgrads), cell_grad[flat_cell])
    state, wgrad, kgrad, obs_grad = lax.map(one_member, (obs_values, obs_tile, obs_cell, backdrop, seed_grad))
    return (state, lax.optimization_barrier(jnp.sum(wgrad, axis=0)), lax.optimization_barrier(jnp.sum(kgrad, axis=0)), obs_grad)
```

```python
import jax
import jax.numpy as jnp
from jax import lax
from jax.experimental import pallas as pl
from jax.experimental.pallas import tpu as pltpu
from jax.sharding import PartitionSpec as P

F32 = jnp.float32
BF16 = jnp.bfloat16
MESH = pl.DeviceIdType.MESH
NX, NY, NZL, NZH, NC = 4, 4, 8, 2, 2
NZ = NZL * NZH


def reduce_kernel(
    w_ref, k_ref, wo_ref, ko_ref,
    c_send, c_recv, x_send, x_recv, y_send, y_recv, z_send, z_recv,
    zg, yg, xg, cg,
    kc_recv, kx_send, kx_recv, ky_send, ky_recv, kyg, kxg,
    c_ss, c_rs, x_ss, x_rs, y_ss, y_rs, z_ss, z_rs, g_ss, g_rs,
    kc_ss, kc_rs, kx_ss, kx_rs, ky_ss, ky_rs, kyg_ss, kyg_rs, kxg_ss, kxg_rs,
    yg_ss, yg_rs, xg_ss, xg_rs, cg_ss, cg_rs,
):
    lon = lax.axis_index("lon")
    x = lax.axis_index("lat")
    ens = lax.axis_index("ens")
    zl, y = lon // NY, lon % NY
    zh, core = ens // NC, ens % NC
    z = zh * NZL + zl

    def at(px, py, pz, pc):
        return {"lon": (pz % NZL) * NY + py, "lat": px, "ens": (pz // NZL) * NC + pc}

    other = at(x, y, z, 1 - core)
    x_peers = [((x + k) % NX, k) for k in range(1, NX)]
    y_peers = [((y + k) % NY, k) for k in range(1, NY)]
    z_peers = [((z + k) % NZ, k) for k in range(1, NZ)]
    g_peers = [(zh * NZL + (zl + k) % NZL, k) for k in range(1, NZL)]

    barrier = pltpu.get_barrier_semaphore()
    greeted = [other]
    greeted += [at(p, y, z, core) for p, _ in x_peers]
    greeted += [at(x, p, z, core) for p, _ in y_peers]
    greeted += [at(x, y, p, core) for p, _ in z_peers]
    for peer in greeted:
        pl.semaphore_signal(barrier, inc=1, device_id=peer, device_id_type=MESH)
    pl.semaphore_wait(barrier, len(greeted))

    def copy(src, dst, ss, rs, peer):
        return pltpu.make_async_remote_copy(
            src_ref=src, dst_ref=dst, send_sem=ss, recv_sem=rs, device_id=peer, device_id_type=MESH
        )

    def go(copies):
        for c in copies:
            c.start()
        return copies

    def done(copies):
        for c in copies:
            c.wait()

    half = c_send.shape[1]
    for c in range(NC):
        c_send[c] = w_ref[c * half : (c + 1) * half].astype(BF16)
    live = go([
        copy(c_send.at[1 - core], c_recv, c_ss, c_rs, other),
        copy(k_ref, kc_recv, kc_ss, kc_rs, other),
    ])
    done(live)
    rows = x_send.shape[1]
    for p in range(NX):
        mine = w_ref[pl.ds(pl.multiple_of(core * half + p * rows, rows), rows)]
        x_send[p] = (mine + c_recv[p * rows : (p + 1) * rows].astype(F32)).astype(BF16)
    kx_send[...] = k_ref[...] + kc_recv[...]
    kx_recv[x] = kx_send[x]
    live = go(
        [copy(x_send.at[p], x_recv.at[x], x_ss.at[k], x_rs.at[k], at(p, y, z, core)) for p, k in x_peers]
        + [copy(kx_send.at[p], kx_recv.at[x], kx_ss.at[k], kx_rs.at[k], at(p, y, z, core)) for p, k in x_peers]
    )
    x_recv[x] = x_send[x]
    done(live)
    rows = y_send.shape[1]
    for p in range(NY):
        part = pl.ds(p * rows, rows)
        total = x_recv[0, part].astype(F32)
        for q in range(1, NX):
            total = total + x_recv[q, part].astype(F32)
        y_send[p] = total.astype(BF16)
    ksum = kx_recv[0] + kx_recv[1] + kx_recv[2] + kx_recv[3]
    for p in range(NY):
        ky_send[p] = ksum[(p // 2) * 8 : (p // 2) * 8 + 8, (p % 2) * 128 : (p % 2) * 128 + 128]
    live = go(
        [copy(y_send.at[p], y_recv.at[y], y_ss.at[k], y_rs.at[k], at(x, p, z, core)) for p, k in y_peers]
        + [copy(ky_send.at[p], ky_recv.at[y], ky_ss.at[k], ky_rs.at[k], at(x, p, z, core)) for p, k in y_peers]
    )
    y_recv[y] = y_send[y]
    ky_recv[y] = ky_send[y]
    done(live)
    total = y_recv[0].astype(F32)
    for q in range(1, NY):
        total = total + y_recv[q].astype(F32)
    ktile = ky_recv[0] + ky_recv[1] + ky_recv[2] + ky_recv[3]
    for p in range(NZL):
        z_send[p, 0] = total[(p // 2) * 8 : (p // 2) * 8 + 8, (p % 2) * 128 : (p % 2) * 128 + 128]
        z_send[p, 1] = ktile
    live = go([
        copy(z_send.at[p % NZL], z_recv.at[z], z_ss.at[k], z_rs.at[k], at(x, y, p, core)) for p, k in z_peers
    ])
    z_recv[z] = z_send[zl]
    done(live)
    both = z_recv[0]
    for q in range(1, NZ):
        both = both + z_recv[q]
    zg[zl] = both[0]
    kyg[y] = both[1]
    live = go([copy(zg.at[zl], zg.at[zl], g_ss.at[k], g_rs.at[k], at(x, y, p, core)) for p, k in g_peers])
    klive = go([
        copy(kyg.at[y], kyg.at[y], kyg_ss.at[k], kyg_rs.at[k], at(x, p, z, core)) for p, k in y_peers
    ])
    done(klive)
    kxg[x] = kyg[...]
    klive = go([
        copy(kyg, kxg.at[x], kxg_ss.at[k], kxg_rs.at[k], at(p, y, z, core)) for p, k in x_peers
    ])
    done(live)
    for p in range(NZL):
        r = (p // 2) * 8
        c = (p % 2) * 128
        y_send[0, r : r + 8, c : c + 128] = zg[p].astype(BF16)
    yg[y] = y_send[0]
    live = go([
        copy(y_send.at[0], yg.at[y], yg_ss.at[k], yg_rs.at[k], at(x, p, z, core)) for p, k in y_peers
    ])
    done(live)
    live = go([
        copy(yg, xg.at[x], xg_ss.at[k], xg_rs.at[k], at(p, y, z, core)) for p, k in x_peers
    ])
    xg[x] = yg[...]
    done(live)
    live = go([copy(xg, cg, cg_ss, cg_rs, other)])
    done(klive)
    for q in range(NX):
        for p in range(NY):
            r = (p // 2) * 8
            c = (p % 2) * 128
            ko_ref[q, r : r + 8, c : c + 128] = kxg[q, p]
    rows = yg.shape[1]
    for q in range(NX):
        for p in range(NY):
            lo = (q * NY + p) * rows
            wo_ref[pl.ds(pl.multiple_of(core * half + lo, rows), rows)] = xg[q, p].astype(F32)
    done(live)
    for q in range(NX):
        for p in range(NY):
            lo = (q * NY + p) * rows
            wo_ref[pl.ds(pl.multiple_of((1 - core) * half + lo, rows), rows)] = cg[q, p].astype(F32)


def reduce_params(wgrad, kgrad):
    layers, depth, channels = wgrad.shape
    taps = kgrad.shape[1]
    rows = layers * depth
    k_pad = jnp.pad(kgrad, ((0, 0), (0, 16 - taps), (0, 0)))
    rx, ry = rows // (NC * NX), rows // (NC * NX * NY)
    V = pltpu.VMEM
    D = pltpu.SemaphoreType.DMA
    w, k = pl.pallas_call(
        reduce_kernel,
        out_shape=(
            jax.ShapeDtypeStruct((rows, channels), F32),
            jax.ShapeDtypeStruct(k_pad.shape, F32),
        ),
        in_specs=[pl.BlockSpec(memory_space=V)] * 2,
        out_specs=(pl.BlockSpec(memory_space=V),) * 2,
        scratch_shapes=[
            V((NC, rows // NC, channels), BF16), V((rows // NC, channels), BF16),
            V((NX, rx, channels), BF16), V((NX, rx, channels), BF16),
            V((NY, ry, channels), BF16), V((NY, ry, channels), BF16),
            V((NZL, 2, 8, 128), F32), V((NZ, 2, 8, 128), F32),
            V((NZL, 8, 128), F32), V((NY, ry, channels), BF16),
            V((NX, NY, ry, channels), BF16), V((NX, NY, ry, channels), BF16),
            V(k_pad.shape, F32), V(k_pad.shape, F32), V(k_pad.shape, F32),
            V((NY, 8, 128), F32), V((NY, 8, 128), F32), V((NY, 8, 128), F32),
            V((NX, NY, 8, 128), F32),
            D, D, D((NX,)), D((NX,)), D((NY,)), D((NY,)), D((NZ,)), D((NZ,)), D((NZL,)), D((NZL,)),
            D, D, D((NX,)), D((NX,)), D((NY,)), D((NY,)), D((NY,)), D((NY,)), D((NX,)), D((NX,)),
            D((NY,)), D((NY,)), D((NX,)), D((NX,)), D, D,
        ],
        compiler_params=pltpu.CompilerParams(collective_id=0, has_side_effects=True),
        name="param_sum",
    )(wgrad.reshape(rows, channels), k_pad)
    return w.reshape(wgrad.shape), k[:, :taps]


def with_halo(block, sides, width):
    for axis, dim, periodic in sides:
        count = lax.axis_size(axis)
        forward = [(i, i + 1) for i in range(count - 1)]
        if periodic:
            forward.append((count - 1, 0))
        backward = [(target, source) for source, target in forward]
        low = lax.ppermute(
            lax.slice_in_dim(block, block.shape[dim] - width, None, axis=dim), axis, forward
        )
        high = lax.ppermute(lax.slice_in_dim(block, 0, width, axis=dim), axis, backward)
        block = jnp.concatenate([low, block, high], axis=dim)
    return block


SIDES = (("lat", 0, False), ("lon", 1, True))


def depthwise(padded, kernel_rows, offset, sign):
    rows = padded.shape[0] - 2
    cols = padded.shape[1] - 2
    accum = jnp.zeros((rows, cols, padded.shape[2]), F32)
    for a in range(3):
        for b in range(3):
            row_off = offset + sign * a
            col_off = offset + sign * b
            accum = accum + kernel_rows[3 * a + b] * padded[
                row_off : row_off + rows, col_off : col_off + cols
            ].astype(F32)
    return accum


def crop(v, n):
    if n == 0:
        return v
    return v[n : v.shape[0] - n, n : v.shape[1] - n]


def on_device(obs_values, obs_tile, obs_cell, backdrop, seed_grad, kernels, weights):
    n_lon = lax.axis_size("lon")
    n_lat = lax.axis_size("lat")
    spatial = n_lon * n_lat
    obs_count = obs_values.shape[1]
    channels = obs_values.shape[2]
    cap = 2 * obs_count // spatial
    lat_rows = backdrop.shape[1]
    lon_cols = backdrop.shape[2]
    n_cells = lat_rows * lon_cols
    n_layers = weights.shape[0]
    inv_scale = 1.0 / float(lax.axis_size("ens") * spatial * n_cells) ** 0.5

    def inside(v, radius):
        row = lax.broadcasted_iota(jnp.int32, (v.shape[0], 1, 1), 0)
        row = row + lax.axis_index("lat") * lat_rows - radius
        return jnp.where((row >= 0) & (row < n_lat * lat_rows), v, jnp.zeros((), v.dtype))

    seed_wide = with_halo(seed_grad[0], tuple(SIDES), n_layers)

    target = obs_tile[0, :, 0]
    matches = (target[:, None] == jnp.arange(spatial, dtype=jnp.int32)[None, :]).astype(BF16)
    order = jnp.arange(obs_count, dtype=jnp.int32)
    before = (order[:, None] > order[None, :]).astype(BF16)
    ahead = jnp.dot(before, matches, preferred_element_type=F32)
    position = jnp.sum(ahead * matches.astype(F32), axis=1).astype(jnp.int32)
    slot_of = target * cap + position
    place = (slot_of[:, None] == jnp.arange(spatial * cap, dtype=jnp.int32)[None, :]).astype(BF16)
    send_values = lax.dot_general(
        place, obs_values[0], (((0,), (0,)), ((), ())), preferred_element_type=F32
    ).astype(BF16)
    lane = jnp.arange(channels, dtype=jnp.int32)[None, :]
    cell_rows = jnp.where(position[:, None] == lane, obs_cell[0][:, None] + 1, 0).astype(BF16)
    send_cells = (
        lax.dot_general(matches, cell_rows, (((0,), (0,)), ((), ())), preferred_element_type=F32) - 1.0
    ).astype(BF16)
    packed = jnp.concatenate(
        [send_values.reshape(spatial, cap, channels), send_cells.reshape(spatial, 1, channels)], axis=1
    )
    got = lax.all_to_all(
        packed[None], ("lon", "lat"), split_axis=1, concat_axis=0, tiled=True
    ).reshape(spatial, cap + 1, channels)
    recv_values = got[:, :cap].reshape(spatial * cap, channels)
    recv_cells = got[:, cap, :cap].astype(jnp.int32).reshape(spatial * cap)
    onehot_mask = recv_cells[None, :] == jnp.arange(n_cells, dtype=jnp.int32)[:, None]
    onehot = onehot_mask.astype(BF16)
    summed = jnp.dot(onehot, recv_values, preferred_element_type=F32)
    counts = jnp.sum(onehot_mask.astype(jnp.int32), axis=1)
    divisor = jnp.maximum(counts, 1).astype(F32)[:, None]
    hidden = (
        (backdrop[0].reshape(n_cells, channels).astype(F32) + summed / divisor)
        .astype(BF16)
        .reshape(lat_rows, lon_cols, channels)
    )
    wide = 2 * n_layers
    hidden = with_halo(hidden, SIDES, wide)
    fields, pre_acts, acts = [], [], []
    for l in range(n_layers):
        radius = wide - 1 - l
        pre = depthwise(hidden, kernels[l], 0, 1)
        act = jax.nn.silu(pre).astype(BF16)
        mixed = jnp.dot(act.reshape(-1, channels), weights[l], preferred_element_type=F32)
        fields.append(crop(hidden, radius))
        pre_acts.append(crop(pre, radius - l - 1))
        acts.append(crop(act, radius).reshape(n_cells, channels))
        if l == n_layers - 1:
            act = crop(act, radius)
            mixed = jnp.dot(act.reshape(-1, channels), weights[l], preferred_element_type=F32)
            state = (crop(hidden, radius + 1).astype(F32) + mixed.reshape(lat_rows, lon_cols, channels)).astype(BF16)
        else:
            hidden = inside(
                (crop(hidden, 1).astype(F32) + mixed.reshape(pre.shape)).astype(BF16), radius
            )
    grad = seed_wide.astype(F32) * inv_scale
    wgrads = [None] * n_layers
    kgrads = [None] * n_layers
    for l in reversed(range(n_layers)):
        radius = l + 1
        grad_bf = grad.astype(BF16)
        wgrads[l] = lax.dot_general(
            acts[l],
            crop(grad_bf, radius).reshape(n_cells, channels),
            (((0,), (0,)), ((), ())),
            preferred_element_type=F32,
        )
        grad_act = lax.dot_general(
            grad_bf.reshape(-1, channels), weights[l], (((1,), (1,)), ((), ())), preferred_element_type=F32
        )
        pre = pre_acts[l]
        sigma = jax.nn.sigmoid(pre)
        grad_pre = inside(
            (grad_act.reshape(pre.shape) * (sigma * (1.0 + pre * (1.0 - sigma)))).astype(BF16), radius
        )
        field = crop(fields[l], 0)
        own = crop(grad_pre, radius).astype(F32)
        taps = []
        for a in range(3):
            for b in range(3):
                taps.append(
                    jnp.sum(own * field[a : a + lat_rows, b : b + lon_cols].astype(F32), axis=(0, 1))
                )
        kgrads[l] = jnp.stack(taps)
        grad = crop(grad, 1) + depthwise(grad_pre, kernels[l], 2, -1)
    cell_grad = (grad.reshape(n_cells, channels) / divisor).astype(BF16)
    slot_grad = lax.dot_general(
        onehot, cell_grad, (((0,), (0,)), ((), ())), preferred_element_type=F32
    ).astype(BF16)
    returned = lax.all_to_all(
        slot_grad.reshape(spatial, 1, cap, channels),
        ("lon", "lat"),
        split_axis=0,
        concat_axis=1,
        tiled=True,
    )
    weight_grad, kernel_grad = reduce_params(jnp.stack(wgrads), jnp.stack(kgrads))
    obs_grad = jnp.dot(
        place, returned.reshape(spatial * cap, channels), preferred_element_type=F32
    ).astype(BF16)
    return (state[None], weight_grad, kernel_grad, obs_grad[None])


def solution(mesh):
    placed = (
        P("ens", ("lon", "lat"), None),
        P("ens", ("lon", "lat"), None),
        P("ens", ("lon", "lat")),
        P("ens", "lat", "lon", None),
        P("ens", "lat", "lon", None),
        P(),
        P(),
    )
    return jax.shard_map(
        on_device,
        mesh=mesh,
        in_specs=placed,
        out_specs=(P("ens", "lat", "lon", None), P(), P(), P("ens", ("lon", "lat"), None)),
        check_vma=False,
    )
```

```python
import jax
import jax.numpy as jnp
from jax import lax
from jax.experimental import pallas as pl
from jax.experimental.pallas import tpu as pltpu
from jax.sharding import PartitionSpec as P

F32 = jnp.float32
BF16 = jnp.bfloat16
MESH = pl.DeviceIdType.MESH
NX, NY, NZL, NZH, NC = 4, 4, 8, 2, 2
NZ = NZL * NZH


def reduce_kernel(
    w_ref, k_ref, wo_ref, ko_ref,
    c_send, c_recv, x_send, x_recv, y_send, y_recv, z_send, z_recv,
    zg, yg, xg, cg,
    kc_recv, kx_send, kx_recv, ky_send, ky_recv, kyg, kxg,
    c_ss, c_rs, x_ss, x_rs, y_ss, y_rs, z_ss, z_rs, g_ss, g_rs,
    kc_ss, kc_rs, kx_ss, kx_rs, ky_ss, ky_rs, kyg_ss, kyg_rs, kxg_ss, kxg_rs,
    yg_ss, yg_rs, xg_ss, xg_rs, cg_ss, cg_rs,
):
    lon = lax.axis_index("lon")
    x = lax.axis_index("lat")
    ens = lax.axis_index("ens")
    zl, y = lon // NY, lon % NY
    zh, core = ens // NC, ens % NC
    z = zh * NZL + zl

    def at(px, py, pz, pc):
        return {"lon": (pz % NZL) * NY + py, "lat": px, "ens": (pz // NZL) * NC + pc}

    other = at(x, y, z, 1 - core)
    x_peers = [((x + k) % NX, k) for k in range(1, NX)]
    y_peers = [((y + k) % NY, k) for k in range(1, NY)]
    z_peers = [((z + k) % NZ, k) for k in range(1, NZ)]
    g_peers = [(zh * NZL + (zl + k) % NZL, k) for k in range(1, NZL)]

    barrier = pltpu.get_barrier_semaphore()
    greeted = [other]
    greeted += [at(p, y, z, core) for p, _ in x_peers]
    greeted += [at(x, p, z, core) for p, _ in y_peers]
    greeted += [at(x, y, p, core) for p, _ in z_peers]
    for peer in greeted:
        pl.semaphore_signal(barrier, inc=1, device_id=peer, device_id_type=MESH)
    pl.semaphore_wait(barrier, len(greeted))

    def copy(src, dst, ss, rs, peer):
        return pltpu.make_async_remote_copy(
            src_ref=src, dst_ref=dst, send_sem=ss, recv_sem=rs, device_id=peer, device_id_type=MESH
        )

    def go(copies):
        for c in copies:
            c.start()
        return copies

    def done(copies):
        for c in copies:
            c.wait()

    half = c_send.shape[1]
    for c in range(NC):
        c_send[c] = w_ref[c * half : (c + 1) * half].astype(BF16)
    live = go([
        copy(c_send.at[1 - core], c_recv, c_ss, c_rs, other),
        copy(k_ref, kc_recv, kc_ss, kc_rs, other),
    ])
    done(live)
    rows = x_send.shape[1]
    for p in range(NX):
        mine = w_ref[pl.ds(pl.multiple_of(core * half + p * rows, rows), rows)]
        x_send[p] = (mine + c_recv[p * rows : (p + 1) * rows].astype(F32)).astype(BF16)
    kx_send[...] = k_ref[...] + kc_recv[...]
    kx_recv[x] = kx_send[x]
    live = go(
        [copy(x_send.at[p], x_recv.at[x], x_ss.at[k], x_rs.at[k], at(p, y, z, core)) for p, k in x_peers]
        + [copy(kx_send.at[p], kx_recv.at[x], kx_ss.at[k], kx_rs.at[k], at(p, y, z, core)) for p, k in x_peers]
    )
    x_recv[x] = x_send[x]
    done(live)
    rows = y_send.shape[1]
    for p in range(NY):
        part = pl.ds(p * rows, rows)
        total = x_recv[0, part].astype(F32)
        for q in range(1, NX):
            total = total + x_recv[q, part].astype(F32)
        y_send[p] = total.astype(BF16)
    ksum = kx_recv[0] + kx_recv[1] + kx_recv[2] + kx_recv[3]
    for p in range(NY):
        ky_send[p] = ksum[(p // 2) * 8 : (p // 2) * 8 + 8, (p % 2) * 128 : (p % 2) * 128 + 128]
    live = go(
        [copy(y_send.at[p], y_recv.at[y], y_ss.at[k], y_rs.at[k], at(x, p, z, core)) for p, k in y_peers]
        + [copy(ky_send.at[p], ky_recv.at[y], ky_ss.at[k], ky_rs.at[k], at(x, p, z, core)) for p, k in y_peers]
    )
    y_recv[y] = y_send[y]
    ky_recv[y] = ky_send[y]
    done(live)
    total = y_recv[0].astype(F32)
    for q in range(1, NY):
        total = total + y_recv[q].astype(F32)
    ktile = ky_recv[0] + ky_recv[1] + ky_recv[2] + ky_recv[3]
    for p in range(NZL):
        z_send[p, 0] = total[(p // 2) * 8 : (p // 2) * 8 + 8, (p % 2) * 128 : (p % 2) * 128 + 128]
        z_send[p, 1] = ktile
    live = go([
        copy(z_send.at[p % NZL], z_recv.at[z], z_ss.at[k], z_rs.at[k], at(x, y, p, core)) for p, k in z_peers
    ])
    z_recv[z] = z_send[zl]
    done(live)
    both = z_recv[0]
    for q in range(1, NZ):
        both = both + z_recv[q]
    zg[zl] = both[0]
    kyg[y] = both[1]
    live = go([copy(zg.at[zl], zg.at[zl], g_ss.at[k], g_rs.at[k], at(x, y, p, core)) for p, k in g_peers])
    klive = go([
        copy(kyg.at[y], kyg.at[y], kyg_ss.at[k], kyg_rs.at[k], at(x, p, z, core)) for p, k in y_peers
    ])
    done(klive)
    kxg[x] = kyg[...]
    klive = go([
        copy(kyg, kxg.at[x], kxg_ss.at[k], kxg_rs.at[k], at(p, y, z, core)) for p, k in x_peers
    ])
    done(live)
    for p in range(NZL):
        r = (p // 2) * 8
        c = (p % 2) * 128
        y_send[0, r : r + 8, c : c + 128] = zg[p].astype(BF16)
    yg[y] = y_send[0]
    live = go([
        copy(y_send.at[0], yg.at[y], yg_ss.at[k], yg_rs.at[k], at(x, p, z, core)) for p, k in y_peers
    ])
    done(live)
    live = go([
        copy(yg, xg.at[x], xg_ss.at[k], xg_rs.at[k], at(p, y, z, core)) for p, k in x_peers
    ])
    xg[x] = yg[...]
    done(live)
    live = go([copy(xg, cg, cg_ss, cg_rs, other)])
    done(klive)
    for q in range(NX):
        for p in range(NY):
            r = (p // 2) * 8
            c = (p % 2) * 128
            ko_ref[q, r : r + 8, c : c + 128] = kxg[q, p]
    rows = yg.shape[1]
    for q in range(NX):
        for p in range(NY):
            lo = (q * NY + p) * rows
            wo_ref[pl.ds(pl.multiple_of(core * half + lo, rows), rows)] = xg[q, p].astype(F32)
    done(live)
    for q in range(NX):
        for p in range(NY):
            lo = (q * NY + p) * rows
            wo_ref[pl.ds(pl.multiple_of((1 - core) * half + lo, rows), rows)] = cg[q, p].astype(F32)


def reduce_params(wgrad, kgrad):
    layers, depth, channels = wgrad.shape
    taps = kgrad.shape[1]
    rows = layers * depth
    k_pad = jnp.pad(kgrad, ((0, 0), (0, 16 - taps), (0, 0)))
    rx, ry = rows // (NC * NX), rows // (NC * NX * NY)
    V = pltpu.VMEM
    D = pltpu.SemaphoreType.DMA
    w, k = pl.pallas_call(
        reduce_kernel,
        out_shape=(
            jax.ShapeDtypeStruct((rows, channels), F32),
            jax.ShapeDtypeStruct(k_pad.shape, F32),
        ),
        in_specs=[pl.BlockSpec(memory_space=V)] * 2,
        out_specs=(pl.BlockSpec(memory_space=V),) * 2,
        scratch_shapes=[
            V((NC, rows // NC, channels), BF16), V((rows // NC, channels), BF16),
            V((NX, rx, channels), BF16), V((NX, rx, channels), BF16),
            V((NY, ry, channels), BF16), V((NY, ry, channels), BF16),
            V((NZL, 2, 8, 128), F32), V((NZ, 2, 8, 128), F32),
            V((NZL, 8, 128), F32), V((NY, ry, channels), BF16),
            V((NX, NY, ry, channels), BF16), V((NX, NY, ry, channels), BF16),
            V(k_pad.shape, F32), V(k_pad.shape, F32), V(k_pad.shape, F32),
            V((NY, 8, 128), F32), V((NY, 8, 128), F32), V((NY, 8, 128), F32),
            V((NX, NY, 8, 128), F32),
            D, D, D((NX,)), D((NX,)), D((NY,)), D((NY,)), D((NZ,)), D((NZ,)), D((NZL,)), D((NZL,)),
            D, D, D((NX,)), D((NX,)), D((NY,)), D((NY,)), D((NY,)), D((NY,)), D((NX,)), D((NX,)),
            D((NY,)), D((NY,)), D((NX,)), D((NX,)), D, D,
        ],
        compiler_params=pltpu.CompilerParams(collective_id=0, has_side_effects=True),
        name="param_sum",
    )(wgrad.reshape(rows, channels), k_pad)
    return w.reshape(wgrad.shape), k[:, :taps]


def route_kernel(
    send_ref, base_ref, seed_ref, wide_ref, seed_out, cells_ref,
    r1, perm, z_send, r2, tile, strip, seed_strip, h_row, h_col, s_row, s_mid, s_end,
    p_ss, p_rs, z_ss, z_rs, h_ss, h_rs, s_ss, s_rs,
):
    lon = lax.axis_index("lon")
    x = lax.axis_index("lat")
    ens = lax.axis_index("ens")
    n_lon = lax.axis_size("lon")
    zl, y = lon // NY, lon % NY
    mine = y * NX + x

    def at(plon, px):
        return {"lon": plon, "lat": px, "ens": ens}

    plane = []
    for k in range(1, NX * NY):
        px, py = (x + k % NX) % NX, (y + k // NX) % NY
        plane.append((py * NX + px, at(zl * NY + py, px), k))
    along = []
    for k in range(1, NZL):
        pz = (zl + k) % NZL
        along.append((pz, at(pz * NY + y, x), k))
    west, east = (lon + n_lon - 1) % n_lon, (lon + 1) % n_lon
    north, south = (x + NX - 1) % NX, (x + 1) % NX
    lats = (south, x, north)

    barrier = pltpu.get_barrier_semaphore()
    greeted = [p for _, p, _ in plane] + [p for _, p, _ in along]
    greeted += [at(lon, north), at(lon, south)] + [at(w, q) for w in (west, east) for q in lats]
    for peer in greeted:
        pl.semaphore_signal(barrier, inc=1, device_id=peer, device_id_type=MESH)
    rows, cols, channels = base_ref.shape
    seed = seed_ref[...].astype(F32)
    seed_strip[0] = seed[:, :8].reshape(rows * 8, channels).astype(BF16)
    seed_strip[1] = seed[:, cols - 8 :].reshape(rows * 8, channels).astype(BF16)
    pl.semaphore_wait(barrier, len(greeted))

    def copy(src, dst, ss, rs, peer):
        return pltpu.make_async_remote_copy(
            src_ref=src, dst_ref=dst, send_sem=ss, recv_sem=rs, device_id=peer, device_id_type=MESH
        )

    def go(copies):
        for c in copies:
            c.start()
        return copies

    def done(copies):
        for c in copies:
            c.wait()

    live = go([copy(send_ref.at[d], r1.at[mine], p_ss.at[k], p_rs.at[k], peer) for d, peer, k in plane])
    edge = s_row.shape[1]
    cut = edge * 8
    seeds = [
        copy(seed_ref.at[rows - edge : rows], s_row.at[0], s_ss.at[0], s_rs.at[0], at(lon, south)),
        copy(seed_ref.at[0:edge], s_row.at[1], s_ss.at[1], s_rs.at[1], at(lon, north)),
    ]
    for side, other in ((0, east), (1, west)):
        src = seed_strip.at[1 - side]
        n = 2 + 3 * side
        seeds += [
            copy(src.at[rows * 8 - cut : rows * 8], s_end.at[side, 0], s_ss.at[n], s_rs.at[n], at(other, south)),
            copy(src, s_mid.at[side], s_ss.at[n + 1], s_rs.at[n + 1], at(other, x)),
            copy(src.at[0:cut], s_end.at[side, 1], s_ss.at[n + 2], s_rs.at[n + 2], at(other, north)),
        ]
    go(seeds)
    r1[mine] = send_ref[mine]
    total = perm.shape[0]
    items = total // (NX * NY * NZL)
    i = lax.broadcasted_iota(jnp.int32, (total, 1), 0)
    pz = i // (items * NX * NY)
    rest = i - pz * (items * NX * NY)
    source = (rest % (NX * NY)) * (items * NZL) + (rest // (NX * NY)) * NZL + pz
    j = lax.broadcasted_iota(jnp.int32, (total, total), 1)
    perm[...] = jnp.where(j == source, 1.0, 0.0).astype(BF16)
    done(live)
    flat = r1[...].astype(F32).reshape(total, channels).astype(BF16)
    z_send[...] = (
        jnp.dot(perm[...], flat, preferred_element_type=F32).astype(BF16).reshape(z_send.shape)
    )
    live = go([copy(z_send.at[p], r2.at[zl], z_ss.at[k], z_rs.at[k], peer) for p, peer, k in along])
    r2[zl] = z_send[zl]
    done(live)
    group = NX * NY
    spatial = group * NZL
    n_cells = rows * cols
    cells = r2[:, (items - 1) * group : items * group].reshape(spatial, channels)
    cells_ref[...] = cells
    cells = cells.astype(F32)
    lane = lax.broadcasted_iota(jnp.int32, (spatial, n_cells), 1).astype(F32)
    ones = jnp.ones((spatial, channels), BF16)
    summed = jnp.zeros((n_cells, channels), F32)
    counts = jnp.zeros((n_cells, channels), F32)
    for p in range(items - 1):
        hot = jnp.where(cells[:, p : p + 1] == lane, 1.0, 0.0).astype(BF16)
        vals = r2[:, p * group : (p + 1) * group].reshape(spatial, channels)
        turn = (((0,), (0,)), ((), ()))
        summed = summed + lax.dot_general(hot, vals, turn, preferred_element_type=F32)
        counts = counts + lax.dot_general(hot, ones, turn, preferred_element_type=F32)
    base = base_ref[...].astype(F32).reshape(n_cells, channels)
    h0 = (base + summed / jnp.maximum(counts, 1.0)).reshape(rows, cols, channels)
    tile[...] = h0.astype(BF16)
    strip[0] = h0[:, :8].reshape(rows * 8, channels).astype(BF16)
    strip[1] = h0[:, cols - 8 :].reshape(rows * 8, channels).astype(BF16)
    halos = []
    for side, other in ((0, east), (1, west)):
        for t, q in enumerate(lats):
            n = 2 + 3 * side + t
            halos.append(copy(strip.at[1 - side], h_col.at[side, t], h_ss.at[n], h_rs.at[n], at(other, q)))
    halos += [
        copy(tile, h_row.at[0], h_ss.at[0], h_rs.at[0], at(lon, south)),
        copy(tile, h_row.at[1], h_ss.at[1], h_rs.at[1], at(lon, north)),
    ]
    go(halos)
    done(seeds)

    def put(out, row, left, mid, right, keep):
        line = jnp.concatenate([left.astype(F32), mid.astype(F32), right.astype(F32)], axis=0)
        if keep is not None:
            line = jnp.where(keep, line, 0.0)
        out[row] = line.astype(BF16)

    has_north, has_south = x > 0, x < NX - 1
    for r in range(edge):
        c = r * 8
        put(seed_out, r, s_end[0, 0].astype(F32)[c : c + 8], s_row[0, r], s_end[1, 0].astype(F32)[c : c + 8], has_north)
        put(
            seed_out, edge + rows + r,
            s_end[0, 1].astype(F32)[c : c + 8], s_row[1, r], s_end[1, 1].astype(F32)[c : c + 8], has_south,
        )
    for r in range(rows):
        c = r * 8
        put(seed_out, edge + r, s_mid[0].astype(F32)[c : c + 8], seed[r], s_mid[1].astype(F32)[c : c + 8], None)
    done(halos)
    left = [h_col[0, t].astype(F32) for t in range(3)]
    right = [h_col[1, t].astype(F32) for t in range(3)]
    for r in range(rows):
        c = r * 8
        put(wide_ref, r, left[0][c : c + 8], h_row[0, r], right[0][c : c + 8], has_north)
        put(wide_ref, rows + r, left[1][c : c + 8], tile[r], right[1][c : c + 8], None)
        put(wide_ref, 2 * rows + r, left[2][c : c + 8], h_row[1, r], right[2][c : c + 8], has_south)


def route(send, base, seed, edge):
    rows, cols, channels = base.shape
    spatial = NX * NY * NZL
    items = send.shape[1] // NZL
    V = pltpu.VMEM
    D = pltpu.SemaphoreType.DMA
    return pl.pallas_call(
        route_kernel,
        out_shape=(
            jax.ShapeDtypeStruct((3 * rows, cols + 16, channels), BF16),
            jax.ShapeDtypeStruct((2 * edge + rows, cols + 16, channels), BF16),
            jax.ShapeDtypeStruct((spatial, channels), BF16),
        ),
        in_specs=[pl.BlockSpec(memory_space=V)] * 3,
        out_specs=(pl.BlockSpec(memory_space=V),) * 3,
        scratch_shapes=[
            V(send.shape, BF16), V((items * spatial, items * spatial), BF16),
            V((NZL, items * NX * NY, channels), BF16), V((NZL, items * NX * NY, channels), BF16),
            V(base.shape, BF16), V((2, rows * 8, channels), BF16), V((2, rows * 8, channels), BF16),
            V((2, rows, cols, channels), BF16), V((2, 3, rows * 8, channels), BF16),
            V((2, edge, cols, channels), BF16), V((2, rows * 8, channels), BF16),
            V((2, 2, edge * 8, channels), BF16),
            D((NX * NY,)), D((NX * NY,)), D((NZL,)), D((NZL,)), D((8,)), D((8,)), D((8,)), D((8,)),
        ],
        compiler_params=pltpu.CompilerParams(collective_id=1, has_side_effects=True),
        name="route",
    )(send, base, seed)


def depthwise(padded, kernel_rows, offset, sign):
    rows = padded.shape[0] - 2
    cols = padded.shape[1] - 2
    accum = jnp.zeros((rows, cols, padded.shape[2]), F32)
    for a in range(3):
        for b in range(3):
            row_off = offset + sign * a
            col_off = offset + sign * b
            accum = accum + kernel_rows[3 * a + b] * padded[
                row_off : row_off + rows, col_off : col_off + cols
            ].astype(F32)
    return accum


def crop(v, n):
    if n == 0:
        return v
    return v[n : v.shape[0] - n, n : v.shape[1] - n]


def on_device(obs_values, obs_tile, obs_cell, backdrop, seed_grad, kernels, weights):
    n_lon = lax.axis_size("lon")
    n_lat = lax.axis_size("lat")
    spatial = n_lon * n_lat
    obs_count = obs_values.shape[1]
    channels = obs_values.shape[2]
    cap = 2 * obs_count // spatial
    lat_rows = backdrop.shape[1]
    lon_cols = backdrop.shape[2]
    n_cells = lat_rows * lon_cols
    n_layers = weights.shape[0]
    inv_scale = 1.0 / float(lax.axis_size("ens") * spatial * n_cells) ** 0.5

    def inside(v, radius):
        row = lax.broadcasted_iota(jnp.int32, (v.shape[0], 1, 1), 0)
        row = row + lax.axis_index("lat") * lat_rows - radius
        return jnp.where((row >= 0) & (row < n_lat * lat_rows), v, jnp.zeros((), v.dtype))

    target = obs_tile[0, :, 0]
    matches = (target[:, None] == jnp.arange(spatial, dtype=jnp.int32)[None, :]).astype(BF16)
    order = jnp.arange(obs_count, dtype=jnp.int32)
    before = (order[:, None] > order[None, :]).astype(BF16)
    ahead = jnp.dot(before, matches, preferred_element_type=F32)
    position = jnp.sum(ahead * matches.astype(F32), axis=1).astype(jnp.int32)
    slot_of = target * cap + position
    place = (slot_of[:, None] == jnp.arange(spatial * cap, dtype=jnp.int32)[None, :]).astype(BF16)
    send_values = lax.dot_general(
        place, obs_values[0], (((0,), (0,)), ((), ())), preferred_element_type=F32
    ).astype(BF16)
    lane = jnp.arange(channels, dtype=jnp.int32)[None, :]
    cell_rows = jnp.where(position[:, None] == lane, obs_cell[0][:, None] + 1, 0).astype(BF16)
    send_cells = (
        lax.dot_general(matches, cell_rows, (((0,), (0,)), ((), ())), preferred_element_type=F32) - 1.0
    ).astype(BF16)
    packed = jnp.concatenate(
        [send_values.reshape(spatial, cap, channels), send_cells.reshape(spatial, 1, channels)], axis=1
    )
    send = packed.reshape(NZL, NX * NY, cap + 1, channels).transpose(1, 2, 0, 3)
    send = send.reshape(NX * NY, (cap + 1) * NZL, channels)
    hidden, seed_wide, cell_out = route(send, backdrop[0], seed_grad[0], n_layers)
    seed_wide = seed_wide[:, 8 - n_layers : 8 + lon_cols + n_layers]
    recv_cells = cell_out[:, :cap].astype(jnp.int32).reshape(spatial * cap)
    onehot_mask = recv_cells[None, :] == jnp.arange(n_cells, dtype=jnp.int32)[:, None]
    onehot = onehot_mask.astype(BF16)
    counts = jnp.sum(onehot_mask.astype(jnp.int32), axis=1)
    divisor = jnp.maximum(counts, 1).astype(F32)[:, None]
    wide = 2 * n_layers
    fields, pre_acts, acts = [], [], []
    for l in range(n_layers):
        radius = wide - 1 - l
        pre = depthwise(hidden, kernels[l], 0, 1)
        act = jax.nn.silu(pre).astype(BF16)
        mixed = jnp.dot(act.reshape(-1, channels), weights[l], preferred_element_type=F32)
        fields.append(crop(hidden, radius))
        pre_acts.append(crop(pre, radius - l - 1))
        acts.append(crop(act, radius).reshape(n_cells, channels))
        if l == n_layers - 1:
            act = crop(act, radius)
            mixed = jnp.dot(act.reshape(-1, channels), weights[l], preferred_element_type=F32)
            state = (crop(hidden, radius + 1).astype(F32) + mixed.reshape(lat_rows, lon_cols, channels)).astype(BF16)
        else:
            hidden = inside(
                (crop(hidden, 1).astype(F32) + mixed.reshape(pre.shape)).astype(BF16), radius
            )
    grad = seed_wide.astype(F32) * inv_scale
    wgrads = [None] * n_layers
    kgrads = [None] * n_layers
    for l in reversed(range(n_layers)):
        radius = l + 1
        grad_bf = grad.astype(BF16)
        wgrads[l] = lax.dot_general(
            acts[l],
            crop(grad_bf, radius).reshape(n_cells, channels),
            (((0,), (0,)), ((), ())),
            preferred_element_type=F32,
        )
        grad_act = lax.dot_general(
            grad_bf.reshape(-1, channels), weights[l], (((1,), (1,)), ((), ())), preferred_element_type=F32
        )
        pre = pre_acts[l]
        sigma = jax.nn.sigmoid(pre)
        grad_pre = inside(
            (grad_act.reshape(pre.shape) * (sigma * (1.0 + pre * (1.0 - sigma)))).astype(BF16), radius
        )
        field = crop(fields[l], 0)
        own = crop(grad_pre, radius).astype(F32)
        taps = []
        for a in range(3):
            for b in range(3):
                taps.append(
                    jnp.sum(own * field[a : a + lat_rows, b : b + lon_cols].astype(F32), axis=(0, 1))
                )
        kgrads[l] = jnp.stack(taps)
        grad = crop(grad, 1) + depthwise(grad_pre, kernels[l], 2, -1)
    cell_grad = (grad.reshape(n_cells, channels) / divisor).astype(BF16)
    slot_grad = lax.dot_general(
        onehot, cell_grad, (((0,), (0,)), ((), ())), preferred_element_type=F32
    ).astype(BF16)
    returned = lax.all_to_all(
        slot_grad.reshape(spatial, 1, cap, channels),
        ("lon", "lat"),
        split_axis=0,
        concat_axis=1,
        tiled=True,
    )
    weight_grad, kernel_grad = reduce_params(jnp.stack(wgrads), jnp.stack(kgrads))
    obs_grad = jnp.dot(
        place, returned.reshape(spatial * cap, channels), preferred_element_type=F32
    ).astype(BF16)
    return (state[None], weight_grad, kernel_grad, obs_grad[None])


def solution(mesh):
    placed = (
        P("ens", ("lon", "lat"), None),
        P("ens", ("lon", "lat"), None),
        P("ens", ("lon", "lat")),
        P("ens", "lat", "lon", None),
        P("ens", "lat", "lon", None),
        P(),
        P(),
    )
    return jax.shard_map(
        on_device,
        mesh=mesh,
        in_specs=placed,
        out_specs=(P("ens", "lat", "lon", None), P(), P(), P("ens", ("lon", "lat"), None)),
        check_vma=False,
    )
```

```python
import jax
import jax.numpy as jnp
from jax import lax
from jax.experimental import pallas as pl
from jax.experimental.pallas import tpu as pltpu
from jax.sharding import PartitionSpec as P

F32 = jnp.float32
BF16 = jnp.bfloat16
MESH = pl.DeviceIdType.MESH
NX, NY, NZL, NZH, NC = 4, 4, 8, 2, 2
NZ = NZL * NZH


def reduce_kernel(
    w_ref, k_ref, wo_ref, ko_ref,
    c_send, c_recv, x_send, x_recv, z_send, z_recv, zg, out, xg, cg,
    kc_recv, kx_send, kx_recv, kxg,
    c_ss, c_rs, x_ss, x_rs, z_ss, z_rs, g_ss, g_rs,
    kc_ss, kc_rs, kx_ss, kx_rs, kxg_ss, kxg_rs, xg_ss, xg_rs, cg_ss, cg_rs,
):
    lon = lax.axis_index("lon")
    x = lax.axis_index("lat")
    ens = lax.axis_index("ens")
    zl, y = lon // NY, lon % NY
    zh, core = ens // NC, ens % NC
    z = zh * NZL + zl
    mine = y * NX + x

    def at(px, py, pz, pc):
        return {"lon": (pz % NZL) * NY + py, "lat": px, "ens": (pz // NZL) * NC + pc}

    other = at(x, y, z, 1 - core)
    plane = []
    for k in range(1, NX * NY):
        px, py = (x + k % NX) % NX, (y + k // NX) % NY
        plane.append((py * NX + px, at(px, py, z, core), k))
    senders = []
    for k in range(1, NX * NY):
        px, py = (x + NX - k % NX) % NX, (y + NY - k // NX) % NY
        senders.append((py * NX + px, k))
    z_peers = [((z + k) % NZ, k) for k in range(1, NZ)]
    g_peers = [(zh * NZL + (zl + k) % NZL, k) for k in range(1, NZL)]

    barrier = pltpu.get_barrier_semaphore()
    greeted = [other] + [p for _, p, _ in plane] + [at(x, y, p, core) for p, _ in z_peers]
    for peer in greeted:
        pl.semaphore_signal(barrier, inc=1, device_id=peer, device_id_type=MESH)
    n, rows = c_send.shape[1], c_send.shape[2]
    half = n * rows
    c_send[...] = w_ref[...].astype(BF16).reshape(c_send.shape)
    pl.semaphore_wait(barrier, len(greeted))

    def copy(src, dst, ss, rs, peer):
        return pltpu.make_async_remote_copy(
            src_ref=src, dst_ref=dst, send_sem=ss, recv_sem=rs, device_id=peer, device_id_type=MESH
        )

    def go(copies):
        for c in copies:
            c.start()
        return copies

    def done(copies):
        for c in copies:
            c.wait()

    order = [(d, k) for d, _, k in plane] + [(mine, 0)]
    first = go([copy(k_ref, kc_recv, kc_ss, kc_rs, other)])
    pieces = go([copy(c_send.at[1 - core, d], c_recv.at[d], c_ss.at[k], c_rs.at[k], other) for d, k in order])
    done(first)
    ksum = k_ref[...] + kc_recv[...]
    for d in range(n):
        r, c = (d // 2) % 2 * 8, d % 2 * 128
        kx_send[d] = ksum[d // 4, r : r + 8, c : c + 128]
    live = go([copy(kx_send.at[d], kx_recv.at[mine], kx_ss.at[k], kx_rs.at[k], peer) for d, peer, k in plane])
    kx_recv[mine] = kx_send[mine]
    for (d, k), piece in zip(order, pieces):
        piece.wait_recv()
        own = w_ref[pl.ds(pl.multiple_of(core * half + d * rows, rows), rows)]
        x_send[d] = (own + c_recv[d].astype(F32)).astype(BF16)
        if k:
            live += go([copy(x_send.at[d], x_recv.at[mine], x_ss.at[k], x_rs.at[k], plane[k - 1][1])])
    x_recv[mine] = x_send[mine]
    for piece in pieces:
        piece.wait_send()
    done(live)
    total = x_recv[0].astype(F32)
    ktile = kx_recv[0]
    for q in range(1, n):
        total = total + x_recv[q].astype(F32)
        ktile = ktile + kx_recv[q]
    for p in range(NZL):
        z_send[p, 0] = total[(p // 2) * 8 : (p // 2) * 8 + 8, (p % 2) * 128 : (p % 2) * 128 + 128]
        z_send[p, 1] = ktile
    live = go([
        copy(z_send.at[p % NZL], z_recv.at[z], z_ss.at[k], z_rs.at[k], at(x, y, p, core)) for p, k in z_peers
    ])
    z_recv[z] = z_send[zl]
    done(live)
    both = z_recv[0]
    for q in range(1, NZ):
        both = both + z_recv[q]
    zg[zl] = both[0]
    kxg[mine] = both[1]
    live = go([copy(zg.at[zl], zg.at[zl], g_ss.at[k], g_rs.at[k], at(x, y, p, core)) for p, k in g_peers])
    klive = go([copy(kxg.at[mine], kxg.at[mine], kxg_ss.at[k], kxg_rs.at[k], peer) for _, peer, k in plane])
    done(live)
    for p in range(NZL):
        r = (p // 2) * 8
        c = (p % 2) * 128
        out[r : r + 8, c : c + 128] = zg[p].astype(BF16)
    live = go([copy(out, xg.at[mine], xg_ss.at[k], xg_rs.at[k], peer) for _, peer, k in plane])
    relay = go([copy(out, cg.at[mine], cg_ss.at[0], cg_rs.at[0], other)])
    xg[mine] = out[...]
    done(klive)
    for d in range(n):
        r, c = (d // 2) % 2 * 8, d % 2 * 128
        ko_ref[d // 4, r : r + 8, c : c + 128] = kxg[d]
    for got, (d, k) in zip(live, senders):
        got.wait_recv()
        relay += go([copy(xg.at[d], cg.at[d], cg_ss.at[k], cg_rs.at[k], other)])
    for got in live:
        got.wait_send()
    for d in range(n):
        wo_ref[pl.ds(pl.multiple_of(core * half + d * rows, rows), rows)] = xg[d].astype(F32)
    done(relay)
    for d in range(n):
        wo_ref[pl.ds(pl.multiple_of((1 - core) * half + d * rows, rows), rows)] = cg[d].astype(F32)


def reduce_params(wgrad, kgrad):
    layers, depth, channels = wgrad.shape
    taps = kgrad.shape[1]
    rows = layers * depth
    k_pad = jnp.pad(kgrad, ((0, 0), (0, 16 - taps), (0, 0)))
    n = NX * NY
    block = (n, rows // (NC * n), channels)
    tiles = (n, 8, 128)
    V = pltpu.VMEM
    D = pltpu.SemaphoreType.DMA
    w, k = pl.pallas_call(
        reduce_kernel,
        out_shape=(
            jax.ShapeDtypeStruct((rows, channels), F32),
            jax.ShapeDtypeStruct(k_pad.shape, F32),
        ),
        in_specs=[pl.BlockSpec(memory_space=V)] * 2,
        out_specs=(pl.BlockSpec(memory_space=V),) * 2,
        scratch_shapes=[
            V((NC,) + block, BF16), V(block, BF16), V(block, BF16), V(block, BF16),
            V((NZL, 2, 8, 128), F32), V((NZ, 2, 8, 128), F32), V((NZL, 8, 128), F32),
            V(block[1:], BF16), V(block, BF16), V(block, BF16),
            V(k_pad.shape, F32), V(tiles, F32), V(tiles, F32), V(tiles, F32),
            D((n,)), D((n,)), D((n,)), D((n,)), D((NZ,)), D((NZ,)), D((NZL,)), D((NZL,)),
            D, D, D((n,)), D((n,)), D((n,)), D((n,)), D((n,)), D((n,)), D((n,)), D((n,)),
        ],
        compiler_params=pltpu.CompilerParams(collective_id=0, has_side_effects=True),
        name="param_sum",
    )(wgrad.reshape(rows, channels), k_pad)
    return w.reshape(wgrad.shape), k[:, :taps]


def route_kernel(
    obs_ref, to_ref, cell_ref, base_ref, seed_ref, wide_ref, seed_out, cells_ref, place_ref,
    send_ref, r1, perm, z_send, r2, tile, strip, seed_strip, h_row, h_col, s_row, s_mid, s_end,
    p_ss, p_rs, z_ss, z_rs, h_ss, h_rs, s_ss, s_rs,
):
    lon = lax.axis_index("lon")
    x = lax.axis_index("lat")
    ens = lax.axis_index("ens")
    n_lon = lax.axis_size("lon")
    zl, y = lon // NY, lon % NY
    mine = y * NX + x

    def at(plon, px):
        return {"lon": plon, "lat": px, "ens": ens}

    plane = []
    for k in range(1, NX * NY):
        px, py = (x + k % NX) % NX, (y + k // NX) % NY
        plane.append((py * NX + px, at(zl * NY + py, px), k))
    along = []
    for k in range(1, NZL):
        pz = (zl + k) % NZL
        along.append((pz, at(pz * NY + y, x), k))
    west, east = (lon + n_lon - 1) % n_lon, (lon + 1) % n_lon
    north, south = (x + NX - 1) % NX, (x + 1) % NX
    lats = (south, x, north)

    barrier = pltpu.get_barrier_semaphore()
    greeted = [p for _, p, _ in plane] + [p for _, p, _ in along]
    greeted += [at(lon, north), at(lon, south)] + [at(w, q) for w in (west, east) for q in lats]
    for peer in greeted:
        pl.semaphore_signal(barrier, inc=1, device_id=peer, device_id_type=MESH)
    rows, cols, channels = base_ref.shape
    seed = seed_ref[...].astype(F32)
    seed_strip[0] = seed[:, :8].reshape(rows * 8, channels).astype(BF16)
    seed_strip[1] = seed[:, cols - 8 :].reshape(rows * 8, channels).astype(BF16)
    total = perm.shape[0]
    items = total // (NX * NY * NZL)
    i = lax.broadcasted_iota(jnp.int32, (total, 1), 0)
    pz = i // (items * NX * NY)
    rest = i - pz * (items * NX * NY)
    source = (rest % (NX * NY)) * (items * NZL) + (rest // (NX * NY)) * NZL + pz
    j = lax.broadcasted_iota(jnp.int32, (total, total), 1)
    perm[...] = jnp.where(j == source, 1.0, 0.0).astype(BF16)
    count = obs_ref.shape[0]
    sub = lax.broadcasted_iota(jnp.int32, (count, count), 0)
    lanes = lax.broadcasted_iota(jnp.int32, (count, count), 1)

    def column(row):
        return jnp.sum(jnp.where(sub == lanes, row.astype(F32), 0.0), axis=1, keepdims=True)

    def lane_of(width):
        return lax.broadcasted_iota(jnp.int32, (count, width), 1).astype(F32)

    def picks(index, width):
        return jnp.where(index == lane_of(width), 1.0, 0.0).astype(BF16)

    group = NX * NY
    spatial = group * NZL
    to = column(to_ref[...])
    cell = column(cell_ref[...])
    matches = picks(to, spatial)
    before = jnp.where(sub > lanes, 1.0, 0.0).astype(BF16)
    ahead = jnp.dot(before, matches, preferred_element_type=F32)
    position = jnp.sum(ahead * matches.astype(F32), axis=1, keepdims=True)
    far = jnp.floor(to * (1.0 / group))
    start = (to - far * group) * (items * NZL) + far
    cell_rows = jnp.where(position == lane_of(channels), cell + 1.0, 0.0).astype(BF16)
    place_ref[...] = picks(to * (items - 1) + position, spatial * (items - 1))
    turn = (((0,), (0,)), ((), ()))
    packed = lax.dot_general(picks(start + position * NZL, total), obs_ref[...], turn, preferred_element_type=F32)
    packed = packed + lax.dot_general(
        picks(start + (items - 1) * NZL, total), cell_rows, turn, preferred_element_type=F32
    )
    packed = packed.reshape(group, items * NZL, channels)
    item = lax.broadcasted_iota(jnp.int32, packed.shape, 1)
    send_ref[...] = jnp.where(item >= (items - 1) * NZL, packed - 1.0, packed).astype(BF16)
    pl.semaphore_wait(barrier, len(greeted))

    def copy(src, dst, ss, rs, peer):
        return pltpu.make_async_remote_copy(
            src_ref=src, dst_ref=dst, send_sem=ss, recv_sem=rs, device_id=peer, device_id_type=MESH
        )

    def go(copies):
        for c in copies:
            c.start()
        return copies

    def done(copies):
        for c in copies:
            c.wait()

    live = go([copy(send_ref.at[d], r1.at[mine], p_ss.at[k], p_rs.at[k], peer) for d, peer, k in plane])
    edge = s_row.shape[1]
    cut = edge * 8
    seeds = [
        copy(seed_ref.at[rows - edge : rows], s_row.at[0], s_ss.at[0], s_rs.at[0], at(lon, south)),
        copy(seed_ref.at[0:edge], s_row.at[1], s_ss.at[1], s_rs.at[1], at(lon, north)),
    ]
    for side, other in ((0, east), (1, west)):
        src = seed_strip.at[1 - side]
        n = 2 + 3 * side
        seeds += [
            copy(src.at[rows * 8 - cut : rows * 8], s_end.at[side, 0], s_ss.at[n], s_rs.at[n], at(other, south)),
            copy(src, s_mid.at[side], s_ss.at[n + 1], s_rs.at[n + 1], at(other, x)),
            copy(src.at[0:cut], s_end.at[side, 1], s_ss.at[n + 2], s_rs.at[n + 2], at(other, north)),
        ]
    go(seeds)
    r1[mine] = send_ref[mine]
    done(live)
    flat = r1[...].astype(F32).reshape(total, channels).astype(BF16)
    z_send[...] = (
        jnp.dot(perm[...], flat, preferred_element_type=F32).astype(BF16).reshape(z_send.shape)
    )
    live = go([copy(z_send.at[p], r2.at[zl], z_ss.at[k], z_rs.at[k], peer) for p, peer, k in along])
    r2[zl] = z_send[zl]
    done(live)
    n_cells = rows * cols
    cells = r2[:, (items - 1) * group : items * group].reshape(spatial, channels)
    cells_ref[...] = cells
    cells = cells.astype(F32)
    lane = lax.broadcasted_iota(jnp.int32, (spatial, n_cells), 1).astype(F32)
    ones = jnp.ones((spatial, channels), BF16)
    summed = jnp.zeros((n_cells, channels), F32)
    counts = jnp.zeros((n_cells, channels), F32)
    for p in range(items - 1):
        hot = jnp.where(cells[:, p : p + 1] == lane, 1.0, 0.0).astype(BF16)
        vals = r2[:, p * group : (p + 1) * group].reshape(spatial, channels)
        summed = summed + lax.dot_general(hot, vals, turn, preferred_element_type=F32)
        counts = counts + lax.dot_general(hot, ones, turn, preferred_element_type=F32)
    base = base_ref[...].astype(F32).reshape(n_cells, channels)
    h0 = (base + summed / jnp.maximum(counts, 1.0)).reshape(rows, cols, channels)
    tile[...] = h0.astype(BF16)
    strip[0] = h0[:, :8].reshape(rows * 8, channels).astype(BF16)
    strip[1] = h0[:, cols - 8 :].reshape(rows * 8, channels).astype(BF16)
    halos = []
    for side, other in ((0, east), (1, west)):
        for t, q in enumerate(lats):
            n = 2 + 3 * side + t
            halos.append(copy(strip.at[1 - side], h_col.at[side, t], h_ss.at[n], h_rs.at[n], at(other, q)))
    halos += [
        copy(tile, h_row.at[0], h_ss.at[0], h_rs.at[0], at(lon, south)),
        copy(tile, h_row.at[1], h_ss.at[1], h_rs.at[1], at(lon, north)),
    ]
    go(halos)
    done(seeds)

    def put(out, row, left, mid, right, keep):
        line = jnp.concatenate([left.astype(F32), mid.astype(F32), right.astype(F32)], axis=0)
        if keep is not None:
            line = jnp.where(keep, line, 0.0)
        out[row] = line.astype(BF16)

    has_north, has_south = x > 0, x < NX - 1
    for r in range(edge):
        c = r * 8
        put(seed_out, r, s_end[0, 0].astype(F32)[c : c + 8], s_row[0, r], s_end[1, 0].astype(F32)[c : c + 8], has_north)
        put(
            seed_out, edge + rows + r,
            s_end[0, 1].astype(F32)[c : c + 8], s_row[1, r], s_end[1, 1].astype(F32)[c : c + 8], has_south,
        )
    for r in range(rows):
        c = r * 8
        put(seed_out, edge + r, s_mid[0].astype(F32)[c : c + 8], seed[r], s_mid[1].astype(F32)[c : c + 8], None)
    done(halos)
    left = [h_col[0, t].astype(F32) for t in range(3)]
    right = [h_col[1, t].astype(F32) for t in range(3)]
    for r in range(rows):
        c = r * 8
        put(wide_ref, r, left[0][c : c + 8], h_row[0, r], right[0][c : c + 8], has_north)
        put(wide_ref, rows + r, left[1][c : c + 8], tile[r], right[1][c : c + 8], None)
        put(wide_ref, 2 * rows + r, left[2][c : c + 8], h_row[1, r], right[2][c : c + 8], has_south)


def route(values, to, cell, base, seed, edge, cap):
    rows, cols, channels = base.shape
    spatial = NX * NY * NZL
    items = cap + 1
    send_shape = (NX * NY, items * NZL, channels)
    V = pltpu.VMEM
    D = pltpu.SemaphoreType.DMA
    return pl.pallas_call(
        route_kernel,
        out_shape=(
            jax.ShapeDtypeStruct((3 * rows, cols + 16, channels), BF16),
            jax.ShapeDtypeStruct((2 * edge + rows, cols + 16, channels), BF16),
            jax.ShapeDtypeStruct((spatial, channels), BF16),
            jax.ShapeDtypeStruct((values.shape[0], spatial * cap), BF16),
        ),
        in_specs=[pl.BlockSpec(memory_space=V)] * 5,
        out_specs=(pl.BlockSpec(memory_space=V),) * 4,
        scratch_shapes=[
            V(send_shape, BF16), V(send_shape, BF16), V((items * spatial, items * spatial), BF16),
            V((NZL, items * NX * NY, channels), BF16), V((NZL, items * NX * NY, channels), BF16),
            V(base.shape, BF16), V((2, rows * 8, channels), BF16), V((2, rows * 8, channels), BF16),
            V((2, rows, cols, channels), BF16), V((2, 3, rows * 8, channels), BF16),
            V((2, edge, cols, channels), BF16), V((2, rows * 8, channels), BF16),
            V((2, 2, edge * 8, channels), BF16),
            D((NX * NY,)), D((NX * NY,)), D((NZL,)), D((NZL,)), D((8,)), D((8,)), D((8,)), D((8,)),
        ],
        compiler_params=pltpu.CompilerParams(collective_id=1, has_side_effects=True),
        name="route",
    )(values, to, cell, base, seed)


def depthwise(padded, kernel_rows, offset, sign):
    rows = padded.shape[0] - 2
    cols = padded.shape[1] - 2
    accum = jnp.zeros((rows, cols, padded.shape[2]), F32)
    for a in range(3):
        for b in range(3):
            row_off = offset + sign * a
            col_off = offset + sign * b
            accum = accum + kernel_rows[3 * a + b] * padded[
                row_off : row_off + rows, col_off : col_off + cols
            ].astype(F32)
    return accum


def crop(v, n):
    if n == 0:
        return v
    return v[n : v.shape[0] - n, n : v.shape[1] - n]


def on_device(obs_values, obs_tile, obs_cell, backdrop, seed_grad, kernels, weights):
    n_lon = lax.axis_size("lon")
    n_lat = lax.axis_size("lat")
    spatial = n_lon * n_lat
    obs_count = obs_values.shape[1]
    channels = obs_values.shape[2]
    cap = 2 * obs_count // spatial
    lat_rows = backdrop.shape[1]
    lon_cols = backdrop.shape[2]
    n_cells = lat_rows * lon_cols
    n_layers = weights.shape[0]
    inv_scale = 1.0 / float(lax.axis_size("ens") * spatial * n_cells) ** 0.5

    def inside(v, radius):
        row = lax.broadcasted_iota(jnp.int32, (v.shape[0], 1, 1), 0)
        row = row + lax.axis_index("lat") * lat_rows - radius
        return jnp.where((row >= 0) & (row < n_lat * lat_rows), v, jnp.zeros((), v.dtype))

    hidden, seed_wide, cell_out, place = route(
        obs_values[0], obs_tile.reshape(1, obs_count), obs_cell, backdrop[0], seed_grad[0], n_layers, cap
    )
    seed_wide = seed_wide[:, 8 - n_layers : 8 + lon_cols + n_layers]
    recv_cells = cell_out[:, :cap].astype(jnp.int32).reshape(spatial * cap)
    onehot_mask = recv_cells[None, :] == jnp.arange(n_cells, dtype=jnp.int32)[:, None]
    onehot = onehot_mask.astype(BF16)
    counts = jnp.sum(onehot_mask.astype(jnp.int32), axis=1)
    divisor = jnp.maximum(counts, 1).astype(F32)[:, None]
    wide = 2 * n_layers
    fields, pre_acts, acts = [], [], []
    for l in range(n_layers):
        radius = wide - 1 - l
        pre = depthwise(hidden, kernels[l], 0, 1)
        act = jax.nn.silu(pre).astype(BF16)
        mixed = jnp.dot(act.reshape(-1, channels), weights[l], preferred_element_type=F32)
        fields.append(crop(hidden, radius))
        pre_acts.append(crop(pre, radius - l - 1))
        acts.append(crop(act, radius).reshape(n_cells, channels))
        if l == n_layers - 1:
            act = crop(act, radius)
            mixed = jnp.dot(act.reshape(-1, channels), weights[l], preferred_element_type=F32)
            state = (crop(hidden, radius + 1).astype(F32) + mixed.reshape(lat_rows, lon_cols, channels)).astype(BF16)
        else:
            hidden = inside(
                (crop(hidden, 1).astype(F32) + mixed.reshape(pre.shape)).astype(BF16), radius
            )
    grad = seed_wide.astype(F32) * inv_scale
    wgrads = [None] * n_layers
    kgrads = [None] * n_layers
    for l in reversed(range(n_layers)):
        radius = l + 1
        grad_bf = grad.astype(BF16)
        wgrads[l] = lax.dot_general(
            acts[l],
            crop(grad_bf, radius).reshape(n_cells, channels),
            (((0,), (0,)), ((), ())),
            preferred_element_type=F32,
        )
        grad_act = lax.dot_general(
            grad_bf.reshape(-1, channels), weights[l], (((1,), (1,)), ((), ())), preferred_element_type=F32
        )
        pre = pre_acts[l]
        sigma = jax.nn.sigmoid(pre)
        grad_pre = inside(
            (grad_act.reshape(pre.shape) * (sigma * (1.0 + pre * (1.0 - sigma)))).astype(BF16), radius
        )
        field = crop(fields[l], 0)
        own = crop(grad_pre, radius).astype(F32)
        taps = []
        for a in range(3):
            for b in range(3):
                taps.append(
                    jnp.sum(own * field[a : a + lat_rows, b : b + lon_cols].astype(F32), axis=(0, 1))
                )
        kgrads[l] = jnp.stack(taps)
        grad = crop(grad, 1) + depthwise(grad_pre, kernels[l], 2, -1)
    cell_grad = (grad.reshape(n_cells, channels) / divisor).astype(BF16)
    slot_grad = lax.dot_general(
        onehot, cell_grad, (((0,), (0,)), ((), ())), preferred_element_type=F32
    ).astype(BF16)
    returned = lax.all_to_all(
        slot_grad.reshape(spatial, 1, cap, channels),
        ("lon", "lat"),
        split_axis=0,
        concat_axis=1,
        tiled=True,
    )
    weight_grad, kernel_grad = reduce_params(jnp.stack(wgrads), jnp.stack(kgrads))
    obs_grad = jnp.dot(
        place, returned.reshape(spatial * cap, channels), preferred_element_type=F32
    ).astype(BF16)
    return (state[None], weight_grad, kernel_grad, obs_grad[None])


def solution(mesh):
    placed = (
        P("ens", ("lon", "lat"), None),
        P("ens", ("lon", "lat"), None),
        P("ens", ("lon", "lat")),
        P("ens", "lat", "lon", None),
        P("ens", "lat", "lon", None),
        P(),
        P(),
    )
    return jax.shard_map(
        on_device,
        mesh=mesh,
        in_specs=placed,
        out_specs=(P("ens", "lat", "lon", None), P(), P(), P("ens", ("lon", "lat"), None)),
        check_vma=False,
    )
```

```python
import functools

import jax
import jax.numpy as jnp
from jax import lax
from jax.experimental import pallas as pl
from jax.experimental.pallas import tpu as pltpu
from jax.sharding import PartitionSpec as P

F32 = jnp.float32
BF16 = jnp.bfloat16
MESH = pl.DeviceIdType.MESH
NX, NY, NZL, NZH, NC = 4, 4, 8, 2, 2
NZ = NZL * NZH


def whole_kernel(
    scale, obs_ref, to_ref, cell_ref, base_ref, seed_ref, k_ref, w_ref,
    state_ref, wo_ref, ko_ref, grad_ref,
    send_ref, r1, perm, z_send, r2, tile, strip, seed_strip, h_row, h_col, s_row, s_mid, s_end,
    place, back, hots, count_ref, hs, ds, ub, own, gs, es, wg, kg, rz_send, rz_recv, rp_send, rp_recv,
    c_send, c_recv, x_send, x_recv, q_send, q_recv, zg, out, xg, cg, kc_recv, kx_send, kx_recv, kxg,
    p_ss, p_rs, z_ss, z_rs, h_ss, h_rs, s_ss, s_rs, b_ss, b_rs, o_ss, o_rs,
    c_ss, c_rs, x_ss, x_rs, q_ss, q_rs, g_ss, g_rs,
    kc_ss, kc_rs, kx_ss, kx_rs, kxg_ss, kxg_rs, xg_ss, xg_rs, cg_ss, cg_rs,
):
    lon = lax.axis_index("lon")
    x = lax.axis_index("lat")
    ens = lax.axis_index("ens")
    n_lon = lax.axis_size("lon")
    zl, y = lon // NY, lon % NY
    mine = y * NX + x

    def at(plon, px):
        return {"lon": plon, "lat": px, "ens": ens}

    plane = []
    for k in range(1, NX * NY):
        px, py = (x + k % NX) % NX, (y + k // NX) % NY
        plane.append((py * NX + px, at(zl * NY + py, px), k))
    along = []
    for k in range(1, NZL):
        pz = (zl + k) % NZL
        along.append((pz, at(pz * NY + y, x), k))
    west, east = (lon + n_lon - 1) % n_lon, (lon + 1) % n_lon
    north, south = (x + NX - 1) % NX, (x + 1) % NX
    lats = (south, x, north)

    barrier = pltpu.get_barrier_semaphore()
    zh, core = ens // NC, ens % NC
    z = zh * NZL + zl

    def dev(pz, pc):
        return {"lon": (pz % NZL) * NY + y, "lat": x, "ens": (pz // NZL) * NC + pc}

    partner = dev(z, 1 - core)
    z_peers = [((z + k) % NZ, k) for k in range(1, NZ)]
    greeted = [partner] + [p for _, p, _ in plane] + [dev(p, core) for p, _ in z_peers]
    greeted += [at(lon, north), at(lon, south)] + [at(w, q) for w in (west, east) for q in lats]
    for peer in greeted:
        pl.semaphore_signal(barrier, inc=1, device_id=peer, device_id_type=MESH)
    rows, cols, channels = base_ref.shape
    seed = seed_ref[...].astype(F32)
    seed_strip[0] = seed[:, :8].reshape(rows * 8, channels).astype(BF16)
    seed_strip[1] = seed[:, cols - 8 :].reshape(rows * 8, channels).astype(BF16)
    total = perm.shape[0]
    items = total // (NX * NY * NZL)
    i = lax.broadcasted_iota(jnp.int32, (total, 1), 0)
    pz = i // (items * NX * NY)
    rest = i - pz * (items * NX * NY)
    source = (rest % (NX * NY)) * (items * NZL) + (rest // (NX * NY)) * NZL + pz
    j = lax.broadcasted_iota(jnp.int32, (total, total), 1)
    perm[...] = jnp.where(j == source, 1.0, 0.0).astype(BF16)
    count = obs_ref.shape[0]
    sub = lax.broadcasted_iota(jnp.int32, (count, count), 0)
    lanes = lax.broadcasted_iota(jnp.int32, (count, count), 1)

    def column(row):
        return jnp.sum(jnp.where(sub == lanes, row.astype(F32), 0.0), axis=1, keepdims=True)

    def lane_of(width):
        return lax.broadcasted_iota(jnp.int32, (count, width), 1).astype(F32)

    def picks(index, width):
        return jnp.where(index == lane_of(width), 1.0, 0.0).astype(BF16)

    group = NX * NY
    spatial = group * NZL
    to = column(to_ref[...])
    cell = column(cell_ref[...])
    matches = picks(to, spatial)
    before = jnp.where(sub > lanes, 1.0, 0.0).astype(BF16)
    ahead = jnp.dot(before, matches, preferred_element_type=F32)
    position = jnp.sum(ahead * matches.astype(F32), axis=1, keepdims=True)
    far = jnp.floor(to * (1.0 / group))
    start = (to - far * group) * (items * NZL) + far
    cell_rows = jnp.where(position == lane_of(channels), cell + 1.0, 0.0).astype(BF16)
    place[...] = picks(
        (to - far * group) * ((items - 1) * NZL) + position * NZL + far, spatial * (items - 1)
    )
    slots = back.shape[0]
    i = lax.broadcasted_iota(jnp.int32, (slots, 1), 0)
    each = (items - 1) * NZL
    source = (i % NZL) * (slots // NZL) + (i % each) // NZL * group + i // each
    j = lax.broadcasted_iota(jnp.int32, (slots, slots), 1)
    back[...] = jnp.where(j == source, 1.0, 0.0).astype(BF16)
    turn = (((0,), (0,)), ((), ()))
    packed = lax.dot_general(picks(start + position * NZL, total), obs_ref[...], turn, preferred_element_type=F32)
    packed = packed + lax.dot_general(
        picks(start + (items - 1) * NZL, total), cell_rows, turn, preferred_element_type=F32
    )
    packed = packed.reshape(group, items * NZL, channels)
    item = lax.broadcasted_iota(jnp.int32, packed.shape, 1)
    send_ref[...] = jnp.where(item >= (items - 1) * NZL, packed - 1.0, packed).astype(BF16)
    pl.semaphore_wait(barrier, len(greeted))

    def copy(src, dst, ss, rs, peer):
        return pltpu.make_async_remote_copy(
            src_ref=src, dst_ref=dst, send_sem=ss, recv_sem=rs, device_id=peer, device_id_type=MESH
        )

    def go(copies):
        for c in copies:
            c.start()
        return copies

    def done(copies):
        for c in copies:
            c.wait()

    live = go([copy(send_ref.at[d], r1.at[mine], p_ss.at[k], p_rs.at[k], peer) for d, peer, k in plane])
    edge = s_row.shape[1]
    cut = edge * 8
    seeds = [
        copy(seed_ref.at[rows - edge : rows], s_row.at[0], s_ss.at[0], s_rs.at[0], at(lon, south)),
        copy(seed_ref.at[0:edge], s_row.at[1], s_ss.at[1], s_rs.at[1], at(lon, north)),
    ]
    for side, other in ((0, east), (1, west)):
        src = seed_strip.at[1 - side]
        n = 2 + 3 * side
        seeds += [
            copy(src.at[rows * 8 - cut : rows * 8], s_end.at[side, 0], s_ss.at[n], s_rs.at[n], at(other, south)),
            copy(src, s_mid.at[side], s_ss.at[n + 1], s_rs.at[n + 1], at(other, x)),
            copy(src.at[0:cut], s_end.at[side, 1], s_ss.at[n + 2], s_rs.at[n + 2], at(other, north)),
        ]
    go(seeds)
    r1[mine] = send_ref[mine]
    done(live)
    flat = r1[...].astype(F32).reshape(total, channels).astype(BF16)
    z_send[...] = (
        jnp.dot(perm[...], flat, preferred_element_type=F32).astype(BF16).reshape(z_send.shape)
    )
    live = go([copy(z_send.at[p], r2.at[zl], z_ss.at[k], z_rs.at[k], peer) for p, peer, k in along])
    r2[zl] = z_send[zl]
    done(live)
    n_cells = rows * cols
    cells = r2[:, (items - 1) * group : items * group].reshape(spatial, channels)
    cells = cells.astype(F32)
    lane = lax.broadcasted_iota(jnp.int32, (spatial, n_cells), 1).astype(F32)
    ones = jnp.ones((spatial, channels), BF16)
    summed = jnp.zeros((n_cells, channels), F32)
    counts = jnp.zeros((n_cells, channels), F32)
    for p in range(items - 1):
        hot = jnp.where(cells[:, p : p + 1] == lane, 1.0, 0.0).astype(BF16)
        hots[p] = hot
        vals = r2[:, p * group : (p + 1) * group].reshape(spatial, channels)
        summed = summed + lax.dot_general(hot, vals, turn, preferred_element_type=F32)
        counts = counts + lax.dot_general(hot, ones, turn, preferred_element_type=F32)
    count_ref[...] = counts
    base = base_ref[...].astype(F32).reshape(n_cells, channels)
    h0 = (base + summed / jnp.maximum(counts, 1.0)).reshape(rows, cols, channels)
    tile[...] = h0.astype(BF16)
    strip[0] = h0[:, :8].reshape(rows * 8, channels).astype(BF16)
    strip[1] = h0[:, cols - 8 :].reshape(rows * 8, channels).astype(BF16)
    halos = []
    for side, other in ((0, east), (1, west)):
        for t, q in enumerate(lats):
            n = 2 + 3 * side + t
            halos.append(copy(strip.at[1 - side], h_col.at[side, t], h_ss.at[n], h_rs.at[n], at(other, q)))
    halos += [
        copy(tile, h_row.at[0], h_ss.at[0], h_rs.at[0], at(lon, south)),
        copy(tile, h_row.at[1], h_ss.at[1], h_rs.at[1], at(lon, north)),
    ]
    go(halos)
    done(seeds)

    def put(dst, row, left, mid, right, keep):
        line = jnp.concatenate([left.astype(F32), mid.astype(F32), right.astype(F32)], axis=0)
        if keep is not None:
            line = jnp.where(keep, line, 0.0)
        dst[row] = line if dst is not gs else line * scale

    has_north, has_south = x > 0, x < NX - 1
    for r in range(edge):
        c = r * 8
        put(gs, r, s_end[0, 0].astype(F32)[c : c + 8], s_row[0, r], s_end[1, 0].astype(F32)[c : c + 8], has_north)
        put(
            gs, edge + rows + r,
            s_end[0, 1].astype(F32)[c : c + 8], s_row[1, r], s_end[1, 1].astype(F32)[c : c + 8], has_south,
        )
    for r in range(rows):
        c = r * 8
        put(gs, edge + r, s_mid[0].astype(F32)[c : c + 8], seed[r], s_mid[1].astype(F32)[c : c + 8], None)
    done(halos)
    first_h = hs.at[0]
    left = [h_col[0, t].astype(F32) for t in range(3)]
    right = [h_col[1, t].astype(F32) for t in range(3)]
    for r in range(rows):
        c = r * 8
        put(first_h, r, left[0][c : c + 8], h_row[0, r], right[0][c : c + 8], has_north)
        put(first_h, rows + r, left[1][c : c + 8], tile[r], right[1][c : c + 8], None)
        put(first_h, 2 * rows + r, left[2][c : c + 8], h_row[1, r], right[2][c : c + 8], has_south)

    layers = w_ref.shape[0]
    width = hs.shape[2]
    tall = hs.shape[1]

    def turned(v, by):
        return pltpu.roll(v, by % width, 0)

    def inside(i, v):
        row = x * rows + i
        return jnp.where((row >= 0) & (row < NX * rows), v, 0.0)

    for l in range(layers):
        lo, hi = l + 1, tall - 1 - l
        taps = [k_ref[l, t : t + 1] for t in range(9)]

        def forward(p, _, l=l, taps=taps):
            lines = [hs[l, p + a - 1] for a in range(3)]
            sums = [taps[b] * lines[0] + taps[3 + b] * lines[1] + taps[6 + b] * lines[2] for b in range(3)]
            d = turned(sums[0], 1) + sums[1] + turned(sums[2], -1)
            ds[l, p] = d
            ub[p] = (d / (1.0 + jnp.exp(-d))).astype(BF16)
            return 0

        lax.fori_loop(lo, hi, forward, 0)
        own[l] = ub[rows : 2 * rows].astype(F32)[:, 8 : 8 + cols].reshape(n_cells, channels).astype(BF16)
        if l == layers - 1:
            mixed = jnp.dot(own[l], w_ref[l], preferred_element_type=F32)
            kept = hs[l, rows : 2 * rows][:, 8 : 8 + cols]
            state_ref[...] = (kept + mixed.reshape(rows, cols, channels)).astype(BF16)
        else:
            step = (hi - lo) // 2

            def mix(t, _, l=l, lo=lo, step=step):
                at_row = lo + t * step
                u = ub[pl.ds(at_row, step)].reshape(step * width, channels)
                mixed = jnp.dot(u, w_ref[l], preferred_element_type=F32).reshape(step, width, channels)
                for q in range(step):
                    new = (hs[l, at_row + q] + mixed[q]).astype(BF16).astype(F32)
                    hs[l + 1, at_row + q] = inside(at_row + q - rows, new)
                return 0

            lax.fori_loop(0, 2, mix, 0)
    shift = rows - edge
    for l in reversed(range(layers)):
        radius = l + 1
        lo, hi = edge - radius, edge + rows + radius
        step = (hi - lo) // 2

        def pull(t, _, l=l, lo=lo, step=step):
            at_row = lo + t * step
            b = gs[pl.ds(at_row, step)].reshape(step * width, channels).astype(BF16)
            ga = lax.dot_general(b, w_ref[l], (((1,), (1,)), ((), ())), preferred_element_type=F32)
            ga = ga.reshape(step, width, channels)
            for q in range(step):
                d = ds[l, at_row + q + shift]
                sig = 1.0 / (1.0 + jnp.exp(-d))
                e = (ga[q] * (sig * (1.0 + d * (1.0 - sig)))).astype(BF16).astype(F32)
                es[at_row + q] = inside(at_row + q - edge, e)
            return 0

        lax.fori_loop(0, 2, pull, 0)
        g_own = gs[edge : edge + rows][:, 8 : 8 + cols].reshape(n_cells, channels).astype(BF16)
        wg[l * channels : (l + 1) * channels] = lax.dot_general(
            own[l], g_own, (((0,), (0,)), ((), ())), preferred_element_type=F32
        )
        col = lax.broadcasted_iota(jnp.int32, (width, channels), 0)
        mid = (col >= 8) & (col < 8 + cols)

        def tap_sums(r, acc, l=l):
            e = jnp.where(mid, es[edge + r], 0.0)
            moved = [turned(e, -1), e, turned(e, 1)]
            new = []
            for t in range(9):
                prod = moved[t % 3] * hs[l, rows + r + t // 3 - 1]
                new.append(acc[t] + jnp.sum(prod.reshape(width // 8, 8, channels), axis=0))
            return tuple(new)

        acc = lax.fori_loop(0, rows, tap_sums, tuple(jnp.zeros((8, channels), F32) for _ in range(9)))
        lines = [jnp.sum(v, axis=0, keepdims=True) for v in acc]
        kg[l] = jnp.concatenate(lines + [jnp.zeros((kg.shape[1] - 9, channels), F32)], axis=0)
        taps = [k_ref[l, t : t + 1] for t in range(9)]

        def spread(q, _, taps=taps):
            lines = [es[q + 1 - a] for a in range(3)]
            sums = [taps[b] * lines[0] + taps[3 + b] * lines[1] + taps[6 + b] * lines[2] for b in range(3)]
            gs[q] = gs[q] + turned(sums[0], -1) + sums[1] + turned(sums[2], 1)
            return 0

        lax.fori_loop(edge - l, edge + rows + l, spread, 0)
    cell_grad = gs[edge : edge + rows][:, 8 : 8 + cols].reshape(n_cells, channels)
    cell_grad = (cell_grad / jnp.maximum(count_ref[...], 1.0)).astype(BF16)
    for p in range(items - 1):
        part = jnp.dot(hots[p], cell_grad, preferred_element_type=F32).astype(BF16)
        rz_send[:, p * group : (p + 1) * group] = part.reshape(NZL, group, channels)
    outward = go([copy(rz_send.at[p], rz_recv.at[zl], b_ss.at[k], b_rs.at[k], peer) for p, peer, k in along])
    rz_recv[zl] = rz_send[zl]
    senders = []
    for k in range(1, NX * NY):
        px, py = (x + NX - k % NX) % NX, (y + NY - k // NX) % NY
        senders.append((py * NX + px, k))
    n, prow = c_send.shape[1], c_send.shape[2]
    half = n * prow
    c_send[...] = wg[...].astype(BF16).reshape(c_send.shape)
    order = [(d, k) for d, _, k in plane] + [(mine, 0)]
    first = go([copy(kg, kc_recv, kc_ss, kc_rs, partner)])
    pieces = go([copy(c_send.at[1 - core, d], c_recv.at[d], c_ss.at[k], c_rs.at[k], partner) for d, k in order])
    done(first)
    ksum = kg[...] + kc_recv[...]
    for d in range(n):
        r, c = (d // 2) % 2 * 8, d % 2 * 128
        kx_send[d] = ksum[d // 4, r : r + 8, c : c + 128]
    live = go([copy(kx_send.at[d], kx_recv.at[mine], kx_ss.at[k], kx_rs.at[k], peer) for d, peer, k in plane])
    kx_recv[mine] = kx_send[mine]
    for (d, k), piece in zip(order, pieces):
        piece.wait_recv()
        own = wg[pl.ds(pl.multiple_of(core * half + d * prow, prow), prow)]
        x_send[d] = (own + c_recv[d].astype(F32)).astype(BF16)
        if k:
            live += go([copy(x_send.at[d], x_recv.at[mine], x_ss.at[k], x_rs.at[k], plane[k - 1][1])])
    x_recv[mine] = x_send[mine]
    for piece in pieces:
        piece.wait_send()
    done(live)
    total = x_recv[0].astype(F32)
    ktile = kx_recv[0]
    for q in range(1, n):
        total = total + x_recv[q].astype(F32)
        ktile = ktile + kx_recv[q]
    for p in range(NZL):
        q_send[p, 0] = total[(p // 2) * 8 : (p // 2) * 8 + 8, (p % 2) * 128 : (p % 2) * 128 + 128]
        q_send[p, 1] = ktile
    live = go([
        copy(q_send.at[p % NZL], q_recv.at[z], q_ss.at[k], q_rs.at[k], dev(p, core)) for p, k in z_peers
    ])
    q_recv[z] = q_send[zl]
    done(outward)
    flat = rz_recv[...].reshape(slots, channels)
    rp_send[...] = jnp.dot(back[...], flat, preferred_element_type=F32).astype(BF16).reshape(rp_send.shape)
    outward = go([copy(rp_send.at[d], rp_recv.at[mine], o_ss.at[k], o_rs.at[k], peer) for d, peer, k in plane])
    rp_recv[mine] = rp_send[mine]
    done(live)
    both = q_recv[0]
    for q in range(1, NZ):
        both = both + q_recv[q]
    zg[zl] = both[0]
    kxg[mine] = both[1]
    live = go([copy(zg.at[zl], zg.at[zl], g_ss.at[k], g_rs.at[k], dev(p, core)) for p, k in [(zh * NZL + (zl + k) % NZL, k) for k in range(1, NZL)]])
    klive = go([copy(kxg.at[mine], kxg.at[mine], kxg_ss.at[k], kxg_rs.at[k], peer) for _, peer, k in plane])
    done(live)
    for p in range(NZL):
        r = (p // 2) * 8
        c = (p % 2) * 128
        out[r : r + 8, c : c + 128] = zg[p].astype(BF16)
    live = go([copy(out, xg.at[mine], xg_ss.at[k], xg_rs.at[k], peer) for _, peer, k in plane])
    relay = go([copy(out, cg.at[mine], cg_ss.at[0], cg_rs.at[0], partner)])
    xg[mine] = out[...]
    done(klive)
    for d in range(n):
        r, c = (d // 2) % 2 * 8, d % 2 * 128
        ko_ref[d // 4, r : r + 8, c : c + 128] = kxg[d]
    for got, (d, k) in zip(live, senders):
        got.wait_recv()
        relay += go([copy(xg.at[d], cg.at[d], cg_ss.at[k], cg_rs.at[k], partner)])
    for got in live:
        got.wait_send()
    done(outward)
    grad_ref[...] = jnp.dot(
        place[...], rp_recv[...].reshape(slots, channels), preferred_element_type=F32
    ).astype(BF16)
    for d in range(n):
        wo_ref[pl.ds(pl.multiple_of(core * half + d * prow, prow), prow)] = xg[d].astype(F32)
    done(relay)
    for d in range(n):
        wo_ref[pl.ds(pl.multiple_of((1 - core) * half + d * prow, prow), prow)] = cg[d].astype(F32)


def on_device(obs_values, obs_tile, obs_cell, backdrop, seed_grad, kernels, weights):
    spatial = lax.axis_size("lon") * lax.axis_size("lat")
    count, channels = obs_values.shape[1:]
    cap = 2 * count // spatial
    items = cap + 1
    rows, cols = backdrop.shape[1:3]
    layers = weights.shape[0]
    edge = layers
    width = cols + 16
    scale = 1.0 / float(lax.axis_size("ens") * spatial * rows * cols) ** 0.5
    group = NX * NY
    depth = layers * channels
    block = (group, depth // (NC * group), channels)
    tiles = (group, 8, 128)
    slots = cap * spatial
    V = pltpu.VMEM
    D = pltpu.SemaphoreType.DMA
    send = (group, items * NZL, channels)
    line = rows * 8
    state, w, k, grad = pl.pallas_call(
        functools.partial(whole_kernel, scale),
        out_shape=(
            jax.ShapeDtypeStruct((rows, cols, channels), BF16),
            jax.ShapeDtypeStruct((depth, channels), F32),
            jax.ShapeDtypeStruct((layers, 16, channels), F32),
            jax.ShapeDtypeStruct((count, channels), BF16),
        ),
        in_specs=[pl.BlockSpec(memory_space=V)] * 7,
        out_specs=(pl.BlockSpec(memory_space=V),) * 4,
        scratch_shapes=[
            V(send, BF16), V(send, BF16), V((items * spatial, items * spatial), BF16),
            V((NZL, items * group, channels), BF16), V((NZL, items * group, channels), BF16),
            V((rows, cols, channels), BF16), V((2, line, channels), BF16), V((2, line, channels), BF16),
            V((2, rows, cols, channels), BF16), V((2, 3, line, channels), BF16),
            V((2, edge, cols, channels), BF16), V((2, line, channels), BF16), V((2, 2, edge * 8, channels), BF16),
            V((count, slots), BF16), V((slots, slots), BF16), V((cap, spatial, rows * cols), BF16),
            V((rows * cols, channels), F32), V((layers, 3 * rows, width, channels), F32),
            V((layers, 3 * rows, width, channels), F32), V((3 * rows, width, channels), BF16),
            V((layers, rows * cols, channels), BF16), V((2 * edge + rows, width, channels), F32),
            V((2 * edge + rows, width, channels), F32), V((depth, channels), F32), V((layers, 16, channels), F32),
            V((NZL, cap * group, channels), BF16), V((NZL, cap * group, channels), BF16),
            V((group, cap * NZL, channels), BF16), V((group, cap * NZL, channels), BF16),
            V((NC,) + block, BF16), V(block, BF16), V(block, BF16), V(block, BF16),
            V((NZL, 2, 8, 128), F32), V((NZ, 2, 8, 128), F32), V((NZL, 8, 128), F32),
            V(block[1:], BF16), V(block, BF16), V(block, BF16),
            V((layers, 16, channels), F32), V(tiles, F32), V(tiles, F32), V(tiles, F32),
            D((group,)), D((group,)), D((NZL,)), D((NZL,)), D((8,)), D((8,)), D((8,)), D((8,)),
            D((NZL,)), D((NZL,)), D((group,)), D((group,)),
            D((group,)), D((group,)), D((group,)), D((group,)), D((NZ,)), D((NZ,)), D((NZL,)), D((NZL,)),
            D, D, D((group,)), D((group,)), D((group,)), D((group,)), D((group,)), D((group,)),
            D((group,)), D((group,)),
        ],
        compiler_params=pltpu.CompilerParams(
            collective_id=0, has_side_effects=True, vmem_limit_bytes=56 * 2**20
        ),
        name="window",
    )(obs_values[0], obs_tile.reshape(1, count), obs_cell, backdrop[0], seed_grad[0], kernels, weights)
    taps = kernels.shape[1]
    return state[None], w.reshape(weights.shape), k[:, :taps], grad[None]


def solution(mesh):
    placed = (
        P("ens", ("lon", "lat"), None),
        P("ens", ("lon", "lat"), None),
        P("ens", ("lon", "lat")),
        P("ens", "lat", "lon", None),
        P("ens", "lat", "lon", None),
        P(),
        P(),
    )
    return jax.shard_map(
        on_device,
        mesh=mesh,
        in_specs=placed,
        out_specs=(P("ens", "lat", "lon", None), P(), P(), P("ens", ("lon", "lat"), None)),
        check_vma=False,
    )
```

```python
import functools

import jax
import jax.numpy as jnp
from jax import lax
from jax.experimental import pallas as pl
from jax.experimental.pallas import tpu as pltpu
from jax.sharding import PartitionSpec as P

F32 = jnp.float32
BF16 = jnp.bfloat16
MESH = pl.DeviceIdType.MESH
NX, NY, NZL, NZH, NC = 4, 4, 8, 2, 2
NZ = NZL * NZH


def whole_kernel(
    scale, obs_ref, to_ref, cell_ref, base_ref, seed_ref, k_ref, w_ref,
    state_ref, wo_ref, ko_ref, grad_ref,
    send_ref, r1, perm, z_send, r2, tile, strip, seed_strip, h_row, h_col, s_row, s_mid, s_end,
    place, back, hots, count_ref, hs, ds, ub, own, gs, es, wg, kg, rz_send, rz_recv, rp_send, rp_recv,
    c_send, c_recv, x_send, x_recv, q_send, q_recv, zg, out, xg, cg, kc_recv, kx_send, kx_recv, kxg,
    p_ss, p_rs, z_ss, z_rs, h_ss, h_rs, s_ss, s_rs, b_ss, b_rs, o_ss, o_rs,
    c_ss, c_rs, x_ss, x_rs, q_ss, q_rs, g_ss, g_rs,
    kc_ss, kc_rs, kx_ss, kx_rs, kxg_ss, kxg_rs, xg_ss, xg_rs, cg_ss, cg_rs,
):
    lon = lax.axis_index("lon")
    x = lax.axis_index("lat")
    ens = lax.axis_index("ens")
    n_lon = lax.axis_size("lon")
    zl, y = lon // NY, lon % NY
    mine = y * NX + x

    def at(plon, px):
        return {"lon": plon, "lat": px, "ens": ens}

    plane = []
    for k in range(1, NX * NY):
        px, py = (x + k % NX) % NX, (y + k // NX) % NY
        plane.append((py * NX + px, at(zl * NY + py, px), k))
    along = []
    for k in range(1, NZL):
        pz = (zl + k) % NZL
        along.append((pz, at(pz * NY + y, x), k))
    west, east = (lon + n_lon - 1) % n_lon, (lon + 1) % n_lon
    north, south = (x + NX - 1) % NX, (x + 1) % NX
    lats = (south, x, north)

    barrier = pltpu.get_barrier_semaphore()
    zh, core = ens // NC, ens % NC
    z = zh * NZL + zl

    def dev(pz, pc):
        return {"lon": (pz % NZL) * NY + y, "lat": x, "ens": (pz // NZL) * NC + pc}

    partner = dev(z, 1 - core)
    z_peers = [((z + k) % NZ, k) for k in range(1, NZ)]
    greeted = [partner] + [p for _, p, _ in plane] + [dev(p, core) for p, _ in z_peers]
    greeted += [at(lon, north), at(lon, south)] + [at(w, q) for w in (west, east) for q in lats]
    for peer in greeted:
        pl.semaphore_signal(barrier, inc=1, device_id=peer, device_id_type=MESH)
    rows, cols, channels = base_ref.shape
    seed = seed_ref[...].astype(F32)
    seed_strip[0] = seed[:, :8].reshape(rows * 8, channels).astype(BF16)
    seed_strip[1] = seed[:, cols - 8 :].reshape(rows * 8, channels).astype(BF16)
    total = perm.shape[0]
    items = total // (NX * NY * NZL)
    i = lax.broadcasted_iota(jnp.int32, (total, 1), 0)
    pz = i // (items * NX * NY)
    rest = i - pz * (items * NX * NY)
    source = (rest % (NX * NY)) * (items * NZL) + (rest // (NX * NY)) * NZL + pz
    j = lax.broadcasted_iota(jnp.int32, (total, total), 1)
    perm[...] = jnp.where(j == source, 1.0, 0.0).astype(BF16)
    count = obs_ref.shape[0]
    sub = lax.broadcasted_iota(jnp.int32, (count, count), 0)
    lanes = lax.broadcasted_iota(jnp.int32, (count, count), 1)

    def column(row):
        return jnp.sum(jnp.where(sub == lanes, row.astype(F32), 0.0), axis=1, keepdims=True)

    def lane_of(width):
        return lax.broadcasted_iota(jnp.int32, (count, width), 1).astype(F32)

    def picks(index, width):
        return jnp.where(index == lane_of(width), 1.0, 0.0).astype(BF16)

    group = NX * NY
    spatial = group * NZL
    to = column(to_ref[...])
    cell = column(cell_ref[...])
    matches = picks(to, spatial)
    before = jnp.where(sub > lanes, 1.0, 0.0).astype(BF16)
    ahead = jnp.dot(before, matches, preferred_element_type=F32)
    position = jnp.sum(ahead * matches.astype(F32), axis=1, keepdims=True)
    far = jnp.floor(to * (1.0 / group))
    start = (to - far * group) * (items * NZL) + far
    cell_rows = jnp.where(position == lane_of(channels), cell + 1.0, 0.0).astype(BF16)
    place[...] = picks(
        (to - far * group) * ((items - 1) * NZL) + position * NZL + far, spatial * (items - 1)
    )
    slots = back.shape[0]
    i = lax.broadcasted_iota(jnp.int32, (slots, 1), 0)
    each = (items - 1) * NZL
    source = (i % NZL) * (slots // NZL) + (i % each) // NZL * group + i // each
    j = lax.broadcasted_iota(jnp.int32, (slots, slots), 1)
    back[...] = jnp.where(j == source, 1.0, 0.0).astype(BF16)
    turn = (((0,), (0,)), ((), ()))
    packed = lax.dot_general(picks(start + position * NZL, total), obs_ref[...], turn, preferred_element_type=F32)
    packed = packed + lax.dot_general(
        picks(start + (items - 1) * NZL, total), cell_rows, turn, preferred_element_type=F32
    )
    packed = packed.reshape(group, items * NZL, channels)
    item = lax.broadcasted_iota(jnp.int32, packed.shape, 1)
    send_ref[...] = jnp.where(item >= (items - 1) * NZL, packed - 1.0, packed).astype(BF16)
    pl.semaphore_wait(barrier, len(greeted))

    def copy(src, dst, ss, rs, peer):
        return pltpu.make_async_remote_copy(
            src_ref=src, dst_ref=dst, send_sem=ss, recv_sem=rs, device_id=peer, device_id_type=MESH
        )

    def go(copies):
        for c in copies:
            c.start()
        return copies

    def done(copies):
        for c in copies:
            c.wait()

    live = go([copy(send_ref.at[d], r1.at[mine], p_ss.at[k], p_rs.at[k], peer) for d, peer, k in plane])
    edge = s_row.shape[1]
    cut = edge * 8
    seeds = [
        copy(seed_ref.at[rows - edge : rows], s_row.at[0], s_ss.at[0], s_rs.at[0], at(lon, south)),
        copy(seed_ref.at[0:edge], s_row.at[1], s_ss.at[1], s_rs.at[1], at(lon, north)),
    ]
    for side, other in ((0, east), (1, west)):
        src = seed_strip.at[1 - side]
        n = 2 + 3 * side
        seeds += [
            copy(src.at[rows * 8 - cut : rows * 8], s_end.at[side, 0], s_ss.at[n], s_rs.at[n], at(other, south)),
            copy(src, s_mid.at[side], s_ss.at[n + 1], s_rs.at[n + 1], at(other, x)),
            copy(src.at[0:cut], s_end.at[side, 1], s_ss.at[n + 2], s_rs.at[n + 2], at(other, north)),
        ]
    go(seeds)
    r1[mine] = send_ref[mine]
    done(live)
    flat = r1[...].astype(F32).reshape(total, channels).astype(BF16)
    z_send[...] = (
        jnp.dot(perm[...], flat, preferred_element_type=F32).astype(BF16).reshape(z_send.shape)
    )
    live = go([copy(z_send.at[p], r2.at[zl], z_ss.at[k], z_rs.at[k], peer) for p, peer, k in along])
    r2[zl] = z_send[zl]
    done(live)
    n_cells = rows * cols
    cells = r2[:, (items - 1) * group : items * group].reshape(spatial, channels)
    cells = cells.astype(F32)
    lane = lax.broadcasted_iota(jnp.int32, (spatial, n_cells), 1).astype(F32)
    ones = jnp.ones((spatial, channels), BF16)
    summed = jnp.zeros((n_cells, channels), F32)
    counts = jnp.zeros((n_cells, channels), F32)
    for p in range(items - 1):
        hot = jnp.where(cells[:, p : p + 1] == lane, 1.0, 0.0).astype(BF16)
        hots[p] = hot
        vals = r2[:, p * group : (p + 1) * group].reshape(spatial, channels)
        summed = summed + lax.dot_general(hot, vals, turn, preferred_element_type=F32)
        counts = counts + lax.dot_general(hot, ones, turn, preferred_element_type=F32)
    count_ref[...] = counts
    base = base_ref[...].astype(F32).reshape(n_cells, channels)
    h0 = (base + summed / jnp.maximum(counts, 1.0)).reshape(rows, cols, channels)
    tile[...] = h0.astype(BF16)
    strip[0] = h0[:, :8].reshape(rows * 8, channels).astype(BF16)
    strip[1] = h0[:, cols - 8 :].reshape(rows * 8, channels).astype(BF16)
    halos = []
    for side, other in ((0, east), (1, west)):
        for t, q in enumerate(lats):
            n = 2 + 3 * side + t
            halos.append(copy(strip.at[1 - side], h_col.at[side, t], h_ss.at[n], h_rs.at[n], at(other, q)))
    halos += [
        copy(tile, h_row.at[0], h_ss.at[0], h_rs.at[0], at(lon, south)),
        copy(tile, h_row.at[1], h_ss.at[1], h_rs.at[1], at(lon, north)),
    ]
    go(halos)
    done(seeds)

    def put(dst, row, left, mid, right, keep):
        line = jnp.concatenate([left.astype(F32), mid.astype(F32), right.astype(F32)], axis=0)
        if keep is not None:
            line = jnp.where(keep, line, 0.0)
        dst[row] = line if dst is not gs else line * scale

    has_north, has_south = x > 0, x < NX - 1
    for r in range(edge):
        c = r * 8
        put(gs, r, s_end[0, 0].astype(F32)[c : c + 8], s_row[0, r], s_end[1, 0].astype(F32)[c : c + 8], has_north)
        put(
            gs, edge + rows + r,
            s_end[0, 1].astype(F32)[c : c + 8], s_row[1, r], s_end[1, 1].astype(F32)[c : c + 8], has_south,
        )
    for r in range(rows):
        c = r * 8
        put(gs, edge + r, s_mid[0].astype(F32)[c : c + 8], seed[r], s_mid[1].astype(F32)[c : c + 8], None)
    done(halos)
    first_h = hs.at[0]
    left = [h_col[0, t].astype(F32) for t in range(3)]
    right = [h_col[1, t].astype(F32) for t in range(3)]
    for r in range(rows):
        c = r * 8
        put(first_h, r, left[0][c : c + 8], h_row[0, r], right[0][c : c + 8], has_north)
        put(first_h, rows + r, left[1][c : c + 8], tile[r], right[1][c : c + 8], None)
        put(first_h, 2 * rows + r, left[2][c : c + 8], h_row[1, r], right[2][c : c + 8], has_south)

    layers = w_ref.shape[0]
    width = hs.shape[2]
    tall = hs.shape[1]

    def turned(v, by):
        return pltpu.roll(v, by % width, 0)

    def inside(i, v):
        row = x * rows + i
        return jnp.where((row >= 0) & (row < NX * rows), v, 0.0)

    for l in range(layers):
        lo, hi = l + 1, tall - 1 - l
        taps = [k_ref[t, l : l + 1] for t in range(9)]

        def forward(p, _, l=l, taps=taps):
            lines = [hs[l, p + a - 1] for a in range(3)]
            sums = [taps[b] * lines[0] + taps[3 + b] * lines[1] + taps[6 + b] * lines[2] for b in range(3)]
            d = turned(sums[0], 1) + sums[1] + turned(sums[2], -1)
            ds[l, p] = d
            ub[p] = (d / (1.0 + jnp.exp(-d))).astype(BF16)
            return 0

        lax.fori_loop(lo, hi, forward, 0)
        own[l] = ub[rows : 2 * rows].astype(F32)[:, 8 : 8 + cols].reshape(n_cells, channels).astype(BF16)
        if l == layers - 1:
            mixed = jnp.dot(own[l], w_ref[l], preferred_element_type=F32)
            kept = hs[l, rows : 2 * rows][:, 8 : 8 + cols]
            state_ref[...] = (kept + mixed.reshape(rows, cols, channels)).astype(BF16)
        else:
            step = (hi - lo) // 2

            def mix(t, _, l=l, lo=lo, step=step):
                at_row = lo + t * step
                u = ub[pl.ds(at_row, step)].reshape(step * width, channels)
                mixed = jnp.dot(u, w_ref[l], preferred_element_type=F32).reshape(step, width, channels)
                for q in range(step):
                    new = (hs[l, at_row + q] + mixed[q]).astype(BF16).astype(F32)
                    hs[l + 1, at_row + q] = inside(at_row + q - rows, new)
                return 0

            lax.fori_loop(0, 2, mix, 0)
    shift = rows - edge
    prow = c_send.shape[1]
    half = channels // NC

    def rows_of(d, c):
        start = d // 4 * channels + c * half + d % 4 * prow
        return pl.ds(pl.multiple_of(start, prow), prow)

    def swap(d):
        return copy(c_send.at[d], c_recv.at[d], c_ss.at[d], c_rs.at[d], partner)

    def hand(l):
        for d in range(4 * l, 4 * l + 4):
            c_send[d] = wg[rows_of(d, 1 - core)].astype(BF16)
            swap(d).start()

    def push(l):
        for d in range(4 * l, 4 * l + 4):
            swap(d).wait()
            x_send[d] = (wg[rows_of(d, core)] + c_recv[d].astype(F32)).astype(BF16)

            @pl.when(mine != d)
            def _(d=d):
                to_peer = at(zl * NY + d // NX, d % NX)
                copy(x_send.at[d], x_recv.at[mine], x_ss.at[d], x_rs.at[mine], to_peer).start()

    for l in reversed(range(layers)):
        radius = l + 1
        lo, hi = edge - radius, edge + rows + radius
        step = (hi - lo) // 2

        def pull(t, _, l=l, lo=lo, step=step):
            at_row = lo + t * step
            b = gs[pl.ds(at_row, step)].reshape(step * width, channels).astype(BF16)
            ga = lax.dot_general(b, w_ref[l], (((1,), (1,)), ((), ())), preferred_element_type=F32)
            ga = ga.reshape(step, width, channels)
            for q in range(step):
                d = ds[l, at_row + q + shift]
                sig = 1.0 / (1.0 + jnp.exp(-d))
                e = (ga[q] * (sig * (1.0 + d * (1.0 - sig)))).astype(BF16).astype(F32)
                es[at_row + q] = inside(at_row + q - edge, e)
            return 0

        lax.fori_loop(0, 2, pull, 0)
        g_own = gs[edge : edge + rows][:, 8 : 8 + cols].reshape(n_cells, channels).astype(BF16)
        wg[l * channels : (l + 1) * channels] = lax.dot_general(
            own[l], g_own, (((0,), (0,)), ((), ())), preferred_element_type=F32
        )
        hand(l)
        if l + 1 < layers:
            push(l + 1)
        col = lax.broadcasted_iota(jnp.int32, (width, channels), 0)
        mid = (col >= 8) & (col < 8 + cols)

        def tap_sums(r, acc, l=l):
            e = jnp.where(mid, es[edge + r], 0.0)
            moved = [turned(e, -1), e, turned(e, 1)]
            new = []
            for t in range(9):
                prod = moved[t % 3] * hs[l, rows + r + t // 3 - 1]
                new.append(acc[t] + jnp.sum(prod.reshape(width // 8, 8, channels), axis=0))
            return tuple(new)

        acc = lax.fori_loop(0, rows, tap_sums, tuple(jnp.zeros((8, channels), F32) for _ in range(9)))
        lines = [jnp.sum(v, axis=0, keepdims=True) for v in acc]
        kg[l] = jnp.concatenate(lines + [jnp.zeros((kg.shape[1] - 9, channels), F32)], axis=0)
        taps = [k_ref[t, l : l + 1] for t in range(9)]

        def spread(q, _, taps=taps):
            lines = [es[q + 1 - a] for a in range(3)]
            sums = [taps[b] * lines[0] + taps[3 + b] * lines[1] + taps[6 + b] * lines[2] for b in range(3)]
            gs[q] = gs[q] + turned(sums[0], -1) + sums[1] + turned(sums[2], 1)
            return 0

        lax.fori_loop(edge - l, edge + rows + l, spread, 0)
    cell_grad = gs[edge : edge + rows][:, 8 : 8 + cols].reshape(n_cells, channels)
    cell_grad = (cell_grad / jnp.maximum(count_ref[...], 1.0)).astype(BF16)
    for p in range(items - 1):
        part = jnp.dot(hots[p], cell_grad, preferred_element_type=F32).astype(BF16)
        rz_send[:, p * group : (p + 1) * group] = part.reshape(NZL, group, channels)
    outward = go([copy(rz_send.at[p], rz_recv.at[zl], b_ss.at[k], b_rs.at[k], peer) for p, peer, k in along])
    rz_recv[zl] = rz_send[zl]
    senders = []
    for k in range(1, NX * NY):
        px, py = (x + NX - k % NX) % NX, (y + NY - k // NX) % NY
        senders.append((py * NX + px, k))
    n = c_send.shape[0]
    first = go([copy(kg, kc_recv, kc_ss, kc_rs, partner)])
    push(0)
    done(first)
    ksum = kg[...] + kc_recv[...]
    for d in range(n):
        r, c = (d // 2) % 2 * 8, d % 2 * 128
        kx_send[d] = ksum[d // 4, r : r + 8, c : c + 128]
    live = go([copy(kx_send.at[d], kx_recv.at[mine], kx_ss.at[k], kx_rs.at[k], peer) for d, peer, k in plane])
    kx_recv[mine] = kx_send[mine]
    x_recv[mine] = x_send[mine]
    live += [copy(x_send.at[d], x_recv.at[d], x_ss.at[d], x_rs.at[d], peer) for d, peer, _ in plane]
    done(live)
    total = x_recv[0].astype(F32)
    ktile = kx_recv[0]
    for q in range(1, n):
        total = total + x_recv[q].astype(F32)
        ktile = ktile + kx_recv[q]
    for p in range(NZL):
        q_send[p, 0] = total[(p // 2) * 8 : (p // 2) * 8 + 8, (p % 2) * 128 : (p % 2) * 128 + 128]
        q_send[p, 1] = ktile
    live = go([
        copy(q_send.at[p % NZL], q_recv.at[z], q_ss.at[k], q_rs.at[k], dev(p, core)) for p, k in z_peers
    ])
    q_recv[z] = q_send[zl]
    done(outward)
    flat = rz_recv[...].reshape(slots, channels)
    rp_send[...] = jnp.dot(back[...], flat, preferred_element_type=F32).astype(BF16).reshape(rp_send.shape)
    outward = go([copy(rp_send.at[d], rp_recv.at[mine], o_ss.at[k], o_rs.at[k], peer) for d, peer, k in plane])
    rp_recv[mine] = rp_send[mine]
    done(live)
    both = q_recv[0]
    for q in range(1, NZ):
        both = both + q_recv[q]
    zg[zl] = both[0]
    kxg[mine] = both[1]
    live = go([copy(zg.at[zl], zg.at[zl], g_ss.at[k], g_rs.at[k], dev(p, core)) for p, k in [(zh * NZL + (zl + k) % NZL, k) for k in range(1, NZL)]])
    klive = go([copy(kxg.at[mine], kxg.at[mine], kxg_ss.at[k], kxg_rs.at[k], peer) for _, peer, k in plane])
    done(live)
    for p in range(NZL):
        r = (p // 2) * 8
        c = (p % 2) * 128
        out[r : r + 8, c : c + 128] = zg[p].astype(BF16)
    live = go([copy(out, xg.at[mine], xg_ss.at[k], xg_rs.at[k], peer) for _, peer, k in plane])
    relay = go([copy(out, cg.at[mine], cg_ss.at[0], cg_rs.at[0], partner)])
    xg[mine] = out[...]
    done(klive)
    for d in range(n):
        r, c = (d // 2) % 2 * 8, d % 2 * 128
        ko_ref[d // 4, r : r + 8, c : c + 128] = kxg[d]
    for got, (d, k) in zip(live, senders):
        got.wait_recv()
        relay += go([copy(xg.at[d], cg.at[d], cg_ss.at[k], cg_rs.at[k], partner)])
    for got in live:
        got.wait_send()
    done(outward)
    grad_ref[...] = jnp.dot(
        place[...], rp_recv[...].reshape(slots, channels), preferred_element_type=F32
    ).astype(BF16)
    for d in range(n):
        wo_ref[rows_of(d, core)] = xg[d]
    done(relay)
    for d in range(n):
        wo_ref[rows_of(d, 1 - core)] = cg[d]


def on_device(obs_values, obs_tile, obs_cell, backdrop, seed_grad, kernels, weights):
    spatial = lax.axis_size("lon") * lax.axis_size("lat")
    count, channels = obs_values.shape[1:]
    cap = 2 * count // spatial
    items = cap + 1
    rows, cols = backdrop.shape[1:3]
    layers = weights.shape[0]
    edge = layers
    width = cols + 16
    scale = 1.0 / float(lax.axis_size("ens") * spatial * rows * cols) ** 0.5
    group = NX * NY
    depth = layers * channels
    block = (group, depth // (NC * group), channels)
    tiles = (group, 8, 128)
    slots = cap * spatial
    V = pltpu.VMEM
    D = pltpu.SemaphoreType.DMA
    send = (group, items * NZL, channels)
    line = rows * 8
    state, w, k, grad = pl.pallas_call(
        functools.partial(whole_kernel, scale),
        out_shape=(
            jax.ShapeDtypeStruct((rows, cols, channels), BF16),
            jax.ShapeDtypeStruct((depth, channels), BF16),
            jax.ShapeDtypeStruct((layers, 16, channels), F32),
            jax.ShapeDtypeStruct((count, channels), BF16),
        ),
        in_specs=[pl.BlockSpec(memory_space=V)] * 7,
        out_specs=(pl.BlockSpec(memory_space=V),) * 4,
        scratch_shapes=[
            V(send, BF16), V(send, BF16), V((items * spatial, items * spatial), BF16),
            V((NZL, items * group, channels), BF16), V((NZL, items * group, channels), BF16),
            V((rows, cols, channels), BF16), V((2, line, channels), BF16), V((2, line, channels), BF16),
            V((2, rows, cols, channels), BF16), V((2, 3, line, channels), BF16),
            V((2, edge, cols, channels), BF16), V((2, line, channels), BF16), V((2, 2, edge * 8, channels), BF16),
            V((count, slots), BF16), V((slots, slots), BF16), V((cap, spatial, rows * cols), BF16),
            V((rows * cols, channels), F32), V((layers, 3 * rows, width, channels), F32),
            V((layers, 3 * rows, width, channels), F32), V((3 * rows, width, channels), BF16),
            V((layers, rows * cols, channels), BF16), V((2 * edge + rows, width, channels), F32),
            V((2 * edge + rows, width, channels), F32), V((depth, channels), F32), V((layers, 16, channels), F32),
            V((NZL, cap * group, channels), BF16), V((NZL, cap * group, channels), BF16),
            V((group, cap * NZL, channels), BF16), V((group, cap * NZL, channels), BF16),
            V(block, BF16), V(block, BF16), V(block, BF16), V(block, BF16),
            V((NZL, 2, 8, 128), F32), V((NZ, 2, 8, 128), F32), V((NZL, 8, 128), F32),
            V(block[1:], BF16), V(block, BF16), V(block, BF16),
            V((layers, 16, channels), F32), V(tiles, F32), V(tiles, F32), V(tiles, F32),
            D((group,)), D((group,)), D((NZL,)), D((NZL,)), D((8,)), D((8,)), D((8,)), D((8,)),
            D((NZL,)), D((NZL,)), D((group,)), D((group,)),
            D((group,)), D((group,)), D((group,)), D((group,)), D((NZ,)), D((NZ,)), D((NZL,)), D((NZL,)),
            D, D, D((group,)), D((group,)), D((group,)), D((group,)), D((group,)), D((group,)),
            D((group,)), D((group,)),
        ],
        compiler_params=pltpu.CompilerParams(
            collective_id=0, has_side_effects=True, vmem_limit_bytes=56 * 2**20
        ),
        name="window",
    )(obs_values[0], obs_tile.reshape(1, count), obs_cell, backdrop[0], seed_grad[0], kernels.transpose(1, 0, 2), weights)
    taps = kernels.shape[1]
    return state[None], w.reshape(weights.shape).astype(F32), k[:, :taps], grad[None]


def solution(mesh):
    placed = (
        P("ens", ("lon", "lat"), None),
        P("ens", ("lon", "lat"), None),
        P("ens", ("lon", "lat")),
        P("ens", "lat", "lon", None),
        P("ens", "lat", "lon", None),
        P(),
        P(),
    )
    return jax.shard_map(
        on_device,
        mesh=mesh,
        in_specs=placed,
        out_specs=(P("ens", "lat", "lon", None), P(), P(), P("ens", ("lon", "lat"), None)),
        check_vma=False,
    )
```

```python
import functools

import jax
import jax.numpy as jnp
from jax import lax
from jax.experimental import pallas as pl
from jax.experimental.pallas import tpu as pltpu
from jax.sharding import PartitionSpec as P

F32 = jnp.float32
BF16 = jnp.bfloat16
MESH = pl.DeviceIdType.MESH
NX, NY, NZL, NZH, NC = 4, 4, 8, 2, 2
NZ = NZL * NZH


def whole_kernel(
    scale, obs_ref, to_ref, cell_ref, base_ref, seed_ref, k_ref, w_ref,
    state_ref, wo_ref, ko_ref, grad_ref,
    send_ref, r1, perm, z_send, r2, tile, strip, seed_strip, h_row, h_col, s_row, s_mid, s_end,
    place, back, hots, count_ref, hs, ds, ub, own, gs, es, wg, kg, rz_send, rz_recv, rp_send, rp_recv,
    c_send, c_recv, x_send, x_recv, q_send, q_recv, zg, out, xg, cg, kc_recv, kx_send, kx_recv, kxg,
    p_ss, p_rs, z_ss, z_rs, h_ss, h_rs, s_ss, s_rs, b_ss, b_rs, o_ss, o_rs,
    c_ss, c_rs, x_ss, x_rs, q_ss, q_rs, g_ss, g_rs,
    kc_ss, kc_rs, kx_ss, kx_rs, kxg_ss, kxg_rs, xg_ss, xg_rs, cg_ss, cg_rs,
):
    lon = lax.axis_index("lon")
    x = lax.axis_index("lat")
    ens = lax.axis_index("ens")
    n_lon = lax.axis_size("lon")
    zl, y = lon // NY, lon % NY
    mine = y * NX + x

    def at(plon, px):
        return {"lon": plon, "lat": px, "ens": ens}

    plane = []
    for k in range(1, NX * NY):
        px, py = (x + k % NX) % NX, (y + k // NX) % NY
        plane.append((py * NX + px, at(zl * NY + py, px), k))
    along = []
    for k in range(1, NZL):
        pz = (zl + k) % NZL
        along.append((pz, at(pz * NY + y, x), k))
    west, east = (lon + n_lon - 1) % n_lon, (lon + 1) % n_lon
    north, south = (x + NX - 1) % NX, (x + 1) % NX
    lats = (south, x, north)

    barrier = pltpu.get_barrier_semaphore()
    zh, core = ens // NC, ens % NC
    z = zh * NZL + zl

    def dev(pz, pc):
        return {"lon": (pz % NZL) * NY + y, "lat": x, "ens": (pz // NZL) * NC + pc}

    partner = dev(z, 1 - core)
    z_peers = [((z + k) % NZ, k) for k in range(1, NZ)]
    greeted = [partner] + [p for _, p, _ in plane] + [dev(p, core) for p, _ in z_peers]
    greeted += [at(lon, north), at(lon, south)] + [at(w, q) for w in (west, east) for q in lats]
    for peer in greeted:
        pl.semaphore_signal(barrier, inc=1, device_id=peer, device_id_type=MESH)
    rows, cols, channels = base_ref.shape
    seed = seed_ref[...].astype(F32)
    seed_strip[0] = seed[:, :8].reshape(rows * 8, channels).astype(BF16)
    seed_strip[1] = seed[:, cols - 8 :].reshape(rows * 8, channels).astype(BF16)
    total = perm.shape[0]
    items = total // (NX * NY * NZL)
    i = lax.broadcasted_iota(jnp.int32, (total, 1), 0)
    pz = i // (items * NX * NY)
    rest = i - pz * (items * NX * NY)
    source = (rest % (NX * NY)) * (items * NZL) + (rest // (NX * NY)) * NZL + pz
    j = lax.broadcasted_iota(jnp.int32, (total, total), 1)
    perm[...] = jnp.where(j == source, 1.0, 0.0).astype(BF16)
    count = obs_ref.shape[0]
    sub = lax.broadcasted_iota(jnp.int32, (count, count), 0)
    lanes = lax.broadcasted_iota(jnp.int32, (count, count), 1)

    def column(row):
        return jnp.sum(jnp.where(sub == lanes, row.astype(F32), 0.0), axis=1, keepdims=True)

    def lane_of(width):
        return lax.broadcasted_iota(jnp.int32, (count, width), 1).astype(F32)

    def picks(index, width):
        return jnp.where(index == lane_of(width), 1.0, 0.0).astype(BF16)

    group = NX * NY
    spatial = group * NZL
    to = column(to_ref[...])
    cell = column(cell_ref[...])
    matches = picks(to, spatial)
    before = jnp.where(sub > lanes, 1.0, 0.0).astype(BF16)
    ahead = jnp.dot(before, matches, preferred_element_type=F32)
    position = jnp.sum(ahead * matches.astype(F32), axis=1, keepdims=True)
    far = jnp.floor(to * (1.0 / group))
    start = (to - far * group) * (items * NZL) + far
    cell_rows = jnp.where(position == lane_of(channels), cell + 1.0, 0.0).astype(BF16)
    place[...] = picks(
        (to - far * group) * ((items - 1) * NZL) + position * NZL + far, spatial * (items - 1)
    )
    slots = back.shape[0]
    i = lax.broadcasted_iota(jnp.int32, (slots, 1), 0)
    each = (items - 1) * NZL
    source = (i % NZL) * (slots // NZL) + (i % each) // NZL * group + i // each
    j = lax.broadcasted_iota(jnp.int32, (slots, slots), 1)
    back[...] = jnp.where(j == source, 1.0, 0.0).astype(BF16)
    turn = (((0,), (0,)), ((), ()))
    packed = lax.dot_general(picks(start + position * NZL, total), obs_ref[...], turn, preferred_element_type=F32)
    packed = packed + lax.dot_general(
        picks(start + (items - 1) * NZL, total), cell_rows, turn, preferred_element_type=F32
    )
    packed = packed.reshape(group, items * NZL, channels)
    item = lax.broadcasted_iota(jnp.int32, packed.shape, 1)
    send_ref[...] = jnp.where(item >= (items - 1) * NZL, packed - 1.0, packed).astype(BF16)
    pl.semaphore_wait(barrier, len(greeted))

    def copy(src, dst, ss, rs, peer):
        return pltpu.make_async_remote_copy(
            src_ref=src, dst_ref=dst, send_sem=ss, recv_sem=rs, device_id=peer, device_id_type=MESH
        )

    def go(copies):
        for c in copies:
            c.start()
        return copies

    def done(copies):
        for c in copies:
            c.wait()

    live = go([copy(send_ref.at[d], r1.at[mine], p_ss.at[k], p_rs.at[k], peer) for d, peer, k in plane])
    edge = s_row.shape[1]
    cut = edge * 8
    seeds = [
        copy(seed_ref.at[rows - edge : rows], s_row.at[0], s_ss.at[0], s_rs.at[0], at(lon, south)),
        copy(seed_ref.at[0:edge], s_row.at[1], s_ss.at[1], s_rs.at[1], at(lon, north)),
    ]
    for side, other in ((0, east), (1, west)):
        src = seed_strip.at[1 - side]
        n = 2 + 3 * side
        seeds += [
            copy(src.at[rows * 8 - cut : rows * 8], s_end.at[side, 0], s_ss.at[n], s_rs.at[n], at(other, south)),
            copy(src, s_mid.at[side], s_ss.at[n + 1], s_rs.at[n + 1], at(other, x)),
            copy(src.at[0:cut], s_end.at[side, 1], s_ss.at[n + 2], s_rs.at[n + 2], at(other, north)),
        ]
    r1[mine] = send_ref[mine]
    done(live)
    flat = r1[...].astype(F32).reshape(total, channels).astype(BF16)
    z_send[...] = (
        jnp.dot(perm[...], flat, preferred_element_type=F32).astype(BF16).reshape(z_send.shape)
    )
    live = go([copy(z_send.at[p], r2.at[zl], z_ss.at[k], z_rs.at[k], peer) for p, peer, k in along])
    go(seeds)
    r2[zl] = z_send[zl]
    done(live)
    n_cells = rows * cols
    cells = r2[:, (items - 1) * group : items * group].reshape(spatial, channels)
    cells = cells.astype(F32)
    lane = lax.broadcasted_iota(jnp.int32, (spatial, n_cells), 1).astype(F32)
    ones = jnp.ones((spatial, channels), BF16)
    summed = jnp.zeros((n_cells, channels), F32)
    counts = jnp.zeros((n_cells, channels), F32)
    for p in range(items - 1):
        hot = jnp.where(cells[:, p : p + 1] == lane, 1.0, 0.0).astype(BF16)
        hots[p] = hot
        vals = r2[:, p * group : (p + 1) * group].reshape(spatial, channels)
        summed = summed + lax.dot_general(hot, vals, turn, preferred_element_type=F32)
        counts = counts + lax.dot_general(hot, ones, turn, preferred_element_type=F32)
    count_ref[...] = counts
    base = base_ref[...].astype(F32).reshape(n_cells, channels)
    h0 = (base + summed / jnp.maximum(counts, 1.0)).reshape(rows, cols, channels)
    tile[...] = h0.astype(BF16)
    strip[0] = h0[:, :8].reshape(rows * 8, channels).astype(BF16)
    strip[1] = h0[:, cols - 8 :].reshape(rows * 8, channels).astype(BF16)
    halos = []
    for side, other in ((0, east), (1, west)):
        for t, q in enumerate(lats):
            n = 2 + 3 * side + t
            halos.append(copy(strip.at[1 - side], h_col.at[side, t], h_ss.at[n], h_rs.at[n], at(other, q)))
    halos += [
        copy(tile, h_row.at[0], h_ss.at[0], h_rs.at[0], at(lon, south)),
        copy(tile, h_row.at[1], h_ss.at[1], h_rs.at[1], at(lon, north)),
    ]
    go(halos)
    done(seeds)

    def put(dst, row, left, mid, right, keep):
        line = jnp.concatenate([left.astype(F32), mid.astype(F32), right.astype(F32)], axis=0)
        if keep is not None:
            line = jnp.where(keep, line, 0.0)
        dst[row] = line if dst is not gs else line * scale

    has_north, has_south = x > 0, x < NX - 1
    for r in range(edge):
        c = r * 8
        put(gs, r, s_end[0, 0].astype(F32)[c : c + 8], s_row[0, r], s_end[1, 0].astype(F32)[c : c + 8], has_north)
        put(
            gs, edge + rows + r,
            s_end[0, 1].astype(F32)[c : c + 8], s_row[1, r], s_end[1, 1].astype(F32)[c : c + 8], has_south,
        )
    for r in range(rows):
        c = r * 8
        put(gs, edge + r, s_mid[0].astype(F32)[c : c + 8], seed[r], s_mid[1].astype(F32)[c : c + 8], None)
    done(halos)
    first_h = hs.at[0]
    left = [h_col[0, t].astype(F32) for t in range(3)]
    right = [h_col[1, t].astype(F32) for t in range(3)]
    for r in range(rows):
        c = r * 8
        put(first_h, r, left[0][c : c + 8], h_row[0, r], right[0][c : c + 8], has_north)
        put(first_h, rows + r, left[1][c : c + 8], tile[r], right[1][c : c + 8], None)
        put(first_h, 2 * rows + r, left[2][c : c + 8], h_row[1, r], right[2][c : c + 8], has_south)

    layers = w_ref.shape[0]
    width = hs.shape[2]
    tall = hs.shape[1]

    def turned(v, by):
        return pltpu.roll(v, by % width, 0)

    def inside(i, v):
        row = x * rows + i
        return jnp.where((row >= 0) & (row < NX * rows), v, 0.0)

    for l in range(layers):
        lo, hi = l + 1, tall - 1 - l
        taps = [k_ref[t, l : l + 1] for t in range(9)]

        def forward(p, _, l=l, taps=taps):
            lines = [hs[l, p + a - 1] for a in range(3)]
            sums = [taps[b] * lines[0] + taps[3 + b] * lines[1] + taps[6 + b] * lines[2] for b in range(3)]
            d = turned(sums[0], 1) + sums[1] + turned(sums[2], -1)
            ds[l, p] = d
            ub[p] = (d / (1.0 + jnp.exp(-d))).astype(BF16)
            return 0

        lax.fori_loop(lo, hi, forward, 0)
        own[l] = ub[rows : 2 * rows].astype(F32)[:, 8 : 8 + cols].reshape(n_cells, channels).astype(BF16)
        if l == layers - 1:
            mixed = jnp.dot(own[l], w_ref[l], preferred_element_type=F32)
            kept = hs[l, rows : 2 * rows][:, 8 : 8 + cols]
            state_ref[...] = (kept + mixed.reshape(rows, cols, channels)).astype(BF16)
        else:
            step = (hi - lo) // 2

            def mix(t, _, l=l, lo=lo, step=step):
                at_row = lo + t * step
                u = ub[pl.ds(at_row, step)].reshape(step * width, channels)
                mixed = jnp.dot(u, w_ref[l], preferred_element_type=F32).reshape(step, width, channels)
                for q in range(step):
                    new = (hs[l, at_row + q] + mixed[q]).astype(BF16).astype(F32)
                    hs[l + 1, at_row + q] = inside(at_row + q - rows, new)
                return 0

            lax.fori_loop(0, 2, mix, 0)
    shift = rows - edge
    prow = c_send.shape[1]
    half = channels // NC

    def rows_of(d, c):
        start = d // 4 * channels + c * half + d % 4 * prow
        return pl.ds(pl.multiple_of(start, prow), prow)

    def swap(d):
        return copy(c_send.at[d], c_recv.at[d], c_ss.at[d], c_rs.at[d], partner)

    def hand(l):
        for d in range(4 * l, 4 * l + 4):
            c_send[d] = wg[rows_of(d, 1 - core)].astype(BF16)
            swap(d).start()

    def push(l):
        for d in range(4 * l, 4 * l + 4):
            swap(d).wait()
            x_send[d] = (wg[rows_of(d, core)] + c_recv[d].astype(F32)).astype(BF16)

            @pl.when(mine != d)
            def _(d=d):
                to_peer = at(zl * NY + d // NX, d % NX)
                copy(x_send.at[d], x_recv.at[mine], x_ss.at[d], x_rs.at[mine], to_peer).start()

    for l in reversed(range(layers)):
        radius = l + 1
        lo, hi = edge - radius, edge + rows + radius
        step = (hi - lo) // 2

        def pull(t, _, l=l, lo=lo, step=step):
            at_row = lo + t * step
            b = gs[pl.ds(at_row, step)].reshape(step * width, channels).astype(BF16)
            ga = lax.dot_general(b, w_ref[l], (((1,), (1,)), ((), ())), preferred_element_type=F32)
            ga = ga.reshape(step, width, channels)
            for q in range(step):
                d = ds[l, at_row + q + shift]
                sig = 1.0 / (1.0 + jnp.exp(-d))
                e = (ga[q] * (sig * (1.0 + d * (1.0 - sig)))).astype(BF16).astype(F32)
                es[at_row + q] = inside(at_row + q - edge, e)
            return 0

        lax.fori_loop(0, 2, pull, 0)
        g_own = gs[edge : edge + rows][:, 8 : 8 + cols].reshape(n_cells, channels).astype(BF16)
        wg[l * channels : (l + 1) * channels] = lax.dot_general(
            own[l], g_own, (((0,), (0,)), ((), ())), preferred_element_type=F32
        )
        hand(l)
        if l + 1 < layers:
            push(l + 1)
        col = lax.broadcasted_iota(jnp.int32, (width, channels), 0)
        mid = (col >= 8) & (col < 8 + cols)

        def tap_sums(r, acc, l=l):
            e = jnp.where(mid, es[edge + r], 0.0)
            moved = [turned(e, -1), e, turned(e, 1)]
            new = []
            for t in range(9):
                prod = moved[t % 3] * hs[l, rows + r + t // 3 - 1]
                new.append(acc[t] + jnp.sum(prod.reshape(width // 8, 8, channels), axis=0))
            return tuple(new)

        acc = lax.fori_loop(0, rows, tap_sums, tuple(jnp.zeros((8, channels), F32) for _ in range(9)))
        lines = [jnp.sum(v, axis=0, keepdims=True) for v in acc]
        kg[l] = jnp.concatenate(lines + [jnp.zeros((kg.shape[1] - 9, channels), F32)], axis=0)
        taps = [k_ref[t, l : l + 1] for t in range(9)]

        def spread(q, _, taps=taps):
            lines = [es[q + 1 - a] for a in range(3)]
            sums = [taps[b] * lines[0] + taps[3 + b] * lines[1] + taps[6 + b] * lines[2] for b in range(3)]
            gs[q] = gs[q] + turned(sums[0], -1) + sums[1] + turned(sums[2], 1)
            return 0

        lax.fori_loop(edge - l, edge + rows + l, spread, 0)
    cell_grad = gs[edge : edge + rows][:, 8 : 8 + cols].reshape(n_cells, channels)
    cell_grad = (cell_grad / jnp.maximum(count_ref[...], 1.0)).astype(BF16)
    for p in range(items - 1):
        part = jnp.dot(hots[p], cell_grad, preferred_element_type=F32).astype(BF16)
        rz_send[:, p * group : (p + 1) * group] = part.reshape(NZL, group, channels)
    outward = go([copy(rz_send.at[p], rz_recv.at[zl], b_ss.at[k], b_rs.at[k], peer) for p, peer, k in along])
    rz_recv[zl] = rz_send[zl]
    senders = []
    for k in range(1, NX * NY):
        px, py = (x + NX - k % NX) % NX, (y + NY - k // NX) % NY
        senders.append((py * NX + px, k))
    n = c_send.shape[0]
    first = go([copy(kg, kc_recv, kc_ss, kc_rs, partner)])
    push(0)
    done(first)
    ksum = kg[...] + kc_recv[...]
    for d in range(n):
        r, c = (d // 2) % 2 * 8, d % 2 * 128
        kx_send[d] = ksum[d // 4, r : r + 8, c : c + 128]
    live = go([copy(kx_send.at[d], kx_recv.at[mine], kx_ss.at[k], kx_rs.at[k], peer) for d, peer, k in plane])
    kx_recv[mine] = kx_send[mine]
    x_recv[mine] = x_send[mine]
    live += [copy(x_send.at[d], x_recv.at[d], x_ss.at[d], x_rs.at[d], peer) for d, peer, _ in plane]
    done(live)
    total = x_recv[0].astype(F32)
    ktile = kx_recv[0]
    for q in range(1, n):
        total = total + x_recv[q].astype(F32)
        ktile = ktile + kx_recv[q]
    for p in range(NZL):
        q_send[p, 0] = total[(p // 2) * 8 : (p // 2) * 8 + 8, (p % 2) * 128 : (p % 2) * 128 + 128]
        q_send[p, 1] = ktile
    live = go([
        copy(q_send.at[p % NZL], q_recv.at[z], q_ss.at[k], q_rs.at[k], dev(p, core)) for p, k in z_peers
    ])
    q_recv[z] = q_send[zl]
    done(outward)
    flat = rz_recv[...].reshape(slots, channels)
    rp_send[...] = jnp.dot(back[...], flat, preferred_element_type=F32).astype(BF16).reshape(rp_send.shape)
    outward = go([copy(rp_send.at[d], rp_recv.at[mine], o_ss.at[k], o_rs.at[k], peer) for d, peer, k in plane])
    rp_recv[mine] = rp_send[mine]
    done(live)
    both = q_recv[0]
    for q in range(1, NZ):
        both = both + q_recv[q]
    zg[zl] = both[0]
    kxg[mine] = both[1]
    live = go([copy(zg.at[zl], zg.at[zl], g_ss.at[k], g_rs.at[k], dev(p, core)) for p, k in [(zh * NZL + (zl + k) % NZL, k) for k in range(1, NZL)]])
    klive = go([copy(kxg.at[mine], kxg.at[mine], kxg_ss.at[k], kxg_rs.at[k], peer) for _, peer, k in plane])
    done(live)
    for p in range(NZL):
        r = (p // 2) * 8
        c = (p % 2) * 128
        out[r : r + 8, c : c + 128] = zg[p].astype(BF16)
    live = go([copy(out, xg.at[mine], xg_ss.at[k], xg_rs.at[k], peer) for _, peer, k in plane])
    relay = go([copy(out, cg.at[mine], cg_ss.at[0], cg_rs.at[0], partner)])
    xg[mine] = out[...]
    done(klive)
    for d in range(n):
        r, c = (d // 2) % 2 * 8, d % 2 * 128
        ko_ref[d // 4, r : r + 8, c : c + 128] = kxg[d]
    for got, (d, k) in zip(live, senders):
        got.wait_recv()
        relay += go([copy(xg.at[d], cg.at[d], cg_ss.at[k], cg_rs.at[k], partner)])
    for got in live:
        got.wait_send()
    done(outward)
    grad_ref[...] = jnp.dot(
        place[...], rp_recv[...].reshape(slots, channels), preferred_element_type=F32
    ).astype(BF16)
    for d in range(n):
        wo_ref[rows_of(d, core)] = xg[d]
    done(relay)
    for d in range(n):
        wo_ref[rows_of(d, 1 - core)] = cg[d]


def on_device(obs_values, obs_tile, obs_cell, backdrop, seed_grad, kernels, weights):
    spatial = lax.axis_size("lon") * lax.axis_size("lat")
    count, channels = obs_values.shape[1:]
    cap = 2 * count // spatial
    items = cap + 1
    rows, cols = backdrop.shape[1:3]
    layers = weights.shape[0]
    edge = layers
    width = cols + 16
    scale = 1.0 / float(lax.axis_size("ens") * spatial * rows * cols) ** 0.5
    group = NX * NY
    depth = layers * channels
    block = (group, depth // (NC * group), channels)
    tiles = (group, 8, 128)
    slots = cap * spatial
    V = pltpu.VMEM
    D = pltpu.SemaphoreType.DMA
    send = (group, items * NZL, channels)
    line = rows * 8
    state, w, k, grad = pl.pallas_call(
        functools.partial(whole_kernel, scale),
        out_shape=(
            jax.ShapeDtypeStruct((rows, cols, channels), BF16),
            jax.ShapeDtypeStruct((depth, channels), BF16),
            jax.ShapeDtypeStruct((layers, 16, channels), F32),
            jax.ShapeDtypeStruct((count, channels), BF16),
        ),
        in_specs=[pl.BlockSpec(memory_space=V)] * 7,
        out_specs=(pl.BlockSpec(memory_space=V),) * 4,
        scratch_shapes=[
            V(send, BF16), V(send, BF16), V((items * spatial, items * spatial), BF16),
            V((NZL, items * group, channels), BF16), V((NZL, items * group, channels), BF16),
            V((rows, cols, channels), BF16), V((2, line, channels), BF16), V((2, line, channels), BF16),
            V((2, rows, cols, channels), BF16), V((2, 3, line, channels), BF16),
            V((2, edge, cols, channels), BF16), V((2, line, channels), BF16), V((2, 2, edge * 8, channels), BF16),
            V((count, slots), BF16), V((slots, slots), BF16), V((cap, spatial, rows * cols), BF16),
            V((rows * cols, channels), F32), V((layers, 3 * rows, width, channels), F32),
            V((layers, 3 * rows, width, channels), F32), V((3 * rows, width, channels), BF16),
            V((layers, rows * cols, channels), BF16), V((2 * edge + rows, width, channels), F32),
            V((2 * edge + rows, width, channels), F32), V((depth, channels), F32), V((layers, 16, channels), F32),
            V((NZL, cap * group, channels), BF16), V((NZL, cap * group, channels), BF16),
            V((group, cap * NZL, channels), BF16), V((group, cap * NZL, channels), BF16),
            V(block, BF16), V(block, BF16), V(block, BF16), V(block, BF16),
            V((NZL, 2, 8, 128), F32), V((NZ, 2, 8, 128), F32), V((NZL, 8, 128), F32),
            V(block[1:], BF16), V(block, BF16), V(block, BF16),
            V((layers, 16, channels), F32), V(tiles, F32), V(tiles, F32), V(tiles, F32),
            D((group,)), D((group,)), D((NZL,)), D((NZL,)), D((8,)), D((8,)), D((8,)), D((8,)),
            D((NZL,)), D((NZL,)), D((group,)), D((group,)),
            D((group,)), D((group,)), D((group,)), D((group,)), D((NZ,)), D((NZ,)), D((NZL,)), D((NZL,)),
            D, D, D((group,)), D((group,)), D((group,)), D((group,)), D((group,)), D((group,)),
            D((group,)), D((group,)),
        ],
        compiler_params=pltpu.CompilerParams(
            collective_id=0, has_side_effects=True, vmem_limit_bytes=56 * 2**20
        ),
        name="window",
    )(obs_values[0], obs_tile.reshape(1, count), obs_cell, backdrop[0], seed_grad[0], kernels.transpose(1, 0, 2), weights)
    taps = kernels.shape[1]
    return state[None], w.reshape(weights.shape).astype(F32), k[:, :taps], grad[None]


def solution(mesh):
    placed = (
        P("ens", ("lon", "lat"), None),
        P("ens", ("lon", "lat"), None),
        P("ens", ("lon", "lat")),
        P("ens", "lat", "lon", None),
        P("ens", "lat", "lon", None),
        P(),
        P(),
    )
    return jax.shard_map(
        on_device,
        mesh=mesh,
        in_specs=placed,
        out_specs=(P("ens", "lat", "lon", None), P(), P(), P("ens", ("lon", "lat"), None)),
        check_vma=False,
    )
```
